32 devices in a mesh: blk: 8 (over z, y), ch: 4 (over x, core).
Axes of the slice: x: 2, y: 2, z: 4, core: 2. Of those that a mesh axis runs over, the one named last changes fastest.
Arguments:
- features: bfloat16 [6144, 512], P('blk', 'ch'), may hold values from -6 to 6
- tile_values: bfloat16 [1024, 128, 128], P('blk'), may hold values from -600 to 600
- tile_source: int32 [1024], P('blk'), may hold values from 0 to 48, as said below
- tile_target: int32 [1024], P('blk'), may hold values from 0 to 5
- tile_count: int32 [8], P('blk'), may hold values from 32 to 128
- weights: bfloat16 [3, 512, 512], replicated, may hold values from -0.15625 to 0.15625
- bias_vector: float32 [512], replicated, may hold values from -3 to 3
Outputs:
- mixed: bfloat16 [6144, 512], P('blk', 'ch')
The draws below stay inside these ranges and needn't reach their ends.
Inputs may be any that keep to these rules, and one draw needn't show every extreme that they name: `tile_source`: in each index of blk the live slots come first, sorted by value, and at most 32 of them name row tiles of one index of blk (tiles 6 * b to 6 * b + 5), a bound that every index of blk reaches; slots from tile_count on hold 48.
All inputs are finite; a program needn't handle non-finite values.
Results may differ from the reference program's by a relative error of at most 0.01.
Values may be sent and summed in bfloat16 or wider, within the bound.
A program may use at most 64 MiB of HBM per device.

```python
import math
import jax
import jax.numpy as jnp
from jax import lax

CHANNELS = 512
TILE = 128
RT_DEV = 6
TILES_DEV = 128
ROWS_DEV = 768
SCAP = 32
GATES = 6144
N_BLK = 8


def pattern(key):
    base_key = jax.random.fold_in(key, 11)
    full_dev = jax.random.randint(jax.random.fold_in(base_key, 1), (), 0, N_BLK)
    low_dev = (full_dev + 1 + jax.random.randint(jax.random.fold_in(base_key, 2), (), 0, N_BLK - 1)) % N_BLK

    def per_device(device):
        device_key = jax.random.fold_in(base_key, 100 + device)
        shuffled = jax.random.permutation(jax.random.fold_in(device_key, 1), (N_BLK - 1) * SCAP).astype(jnp.int32)
        lead_block = jax.random.randint(jax.random.fold_in(device_key, 2), (), 0, N_BLK).astype(jnp.int32)
        others = shuffled[:TILES_DEV - SCAP] // SCAP
        others = others + (others >= lead_block).astype(jnp.int32)
        blocks = jnp.concatenate([jnp.full((SCAP,), lead_block, jnp.int32), others])
        within = jax.random.randint(jax.random.fold_in(device_key, 3), (TILES_DEV,), 0, RT_DEV).astype(jnp.int32)
        halving = jax.random.randint(jax.random.fold_in(device_key, 4), (), 0, 2).astype(jnp.int32)
        live_count = jnp.right_shift(jnp.int32(TILES_DEV), halving)
        live_count = jnp.where(device == full_dev, TILES_DEV, jnp.where(device == low_dev, TILES_DEV // 4, live_count)).astype(jnp.int32)
        usable = jnp.arange(TILES_DEV, dtype=jnp.int32) < live_count
        sort_keys = jnp.where(usable, blocks * RT_DEV + within, N_BLK * RT_DEV).astype(jnp.int32)
        return (jnp.sort(sort_keys), live_count)
    sources, counts = jax.vmap(per_device)(jnp.arange(N_BLK, dtype=jnp.int32))
    return (sources.reshape(-1).astype(jnp.int32), counts.astype(jnp.int32))


def draw_tile_source(key, part):
    return pattern(key)[0]


def draw_tile_count(key, part):
    return pattern(key)[1]


def draw_tile_values(key, part):
    shape = (N_BLK * TILES_DEV, TILE, TILE)
    base_part = jnp.clip(jax.random.normal(jax.random.fold_in(key, 1), shape, jnp.float32), -6.0, 6.0)
    log_top = math.log(10.0)
    row_scale = jnp.exp(jax.random.uniform(jax.random.fold_in(key, 2), (N_BLK * TILES_DEV, TILE, 1), jnp.float32, 0.0, log_top))
    col_scale = jnp.exp(jax.random.uniform(jax.random.fold_in(key, 3), (N_BLK * TILES_DEV, 1, TILE), jnp.float32, 0.0, log_top))
    return jnp.clip(base_part * row_scale * col_scale, -600.0, 600.0).astype(jnp.bfloat16)


def place_ends(array, key, least, largest):
    longest = array.shape.index(max(array.shape))
    spots = []
    for shift in (0, 1):
        where = [jax.random.randint(jax.random.fold_in(key, axis), (), 0, length) for axis, length in enumerate(array.shape)]
        where[longest] = (where[longest] + shift) % array.shape[longest]
        spots.append(tuple(where))
    return array.at[spots[0]].set(least).at[spots[1]].set(largest)


def levels(own_key, extent, pieces, smallest, top_value):
    gain = 1.0
    for axis_at, blocks in pieces:
        draws = jax.random.uniform(jax.random.fold_in(jax.random.fold_in(own_key, 6), axis_at), (blocks,), jnp.float32, smallest / len(pieces), top_value / len(pieces))
        gain = gain * jnp.repeat(jnp.exp(draws), extent[axis_at] // blocks).reshape((-1,) + (1,) * (len(extent) - 1 - axis_at))
    return gain


def scatter_about(key, extent, scale, limit, shards=(), kind=jnp.bfloat16):
    entries = jax.random.normal(key, extent, jnp.float32) * scale
    if len(shards) > 0:
        entries = levels(key, extent, shards, -0.22, 0.18) * entries
    return jnp.clip(entries, min=-limit, max=limit).astype(kind)


def setup_inputs(seed: int = 0) -> dict:
    keys = jax.random.split(jax.random.key(seed), 8)
    return {
        "features": scatter_about(keys[0], (GATES, CHANNELS), 1.0, 6.0, ((0, 8), (1, 4))),
        "tile_values": draw_tile_values(jax.random.fold_in(keys[7], 71), 0),
        "tile_source": draw_tile_source(jax.random.fold_in(keys[7], 71), 0),
        "tile_target": place_ends(jax.random.randint(keys[3], (N_BLK * TILES_DEV,), 0, RT_DEV), jax.random.fold_in(keys[3], 1), 0, RT_DEV - 1).astype(jnp.int32),
        "tile_count": draw_tile_count(jax.random.fold_in(keys[7], 71), 0),
        "weights": scatter_about(keys[5], (3, CHANNELS, CHANNELS), (3 * CHANNELS) ** -0.5, 0.15625),
        "bias_vector": scatter_about(keys[6], (CHANNELS,), 0.5, 3.0, (), jnp.float32),
    }


def propagate(signal, tile_values, tile_source, tile_target, tile_count):
    blocks = signal.reshape(N_BLK * RT_DEV, TILE, CHANNELS)

    def per_device(device):
        first_tile = (device * TILES_DEV).astype(jnp.int32)
        values = lax.dynamic_slice_in_dim(tile_values, first_tile, TILES_DEV, 0).astype(jnp.float32)
        source = lax.dynamic_slice_in_dim(tile_source, first_tile, TILES_DEV, 0)
        target = lax.dynamic_slice_in_dim(tile_target, first_tile, TILES_DEV, 0)
        usable = jnp.arange(TILES_DEV, dtype=jnp.int32) < tile_count[device]
        picked = blocks[jnp.where(usable, source, 0)].astype(jnp.float32)
        product = jnp.einsum('tij,tjc->tic', values, picked, precision=lax.Precision.HIGHEST)
        product = jnp.where(usable[:, None, None], product, jnp.float32(0.0))
        running = jnp.zeros((RT_DEV, TILE, CHANNELS), jnp.float32).at[target].add(product)
        squares = jnp.where(usable[:, None], lax.optimization_barrier(jnp.sum(values * values, axis=2)), jnp.float32(0.0))
        row_norm = jnp.zeros((RT_DEV, TILE), jnp.float32).at[target].add(squares)
        return running * lax.rsqrt(1.0 + row_norm)[:, :, None]
    stacked_out = lax.map(per_device, jnp.arange(N_BLK, dtype=jnp.int32))
    return stacked_out.reshape(N_BLK * ROWS_DEV, CHANNELS)

def reference(features, tile_values, tile_source, tile_target, tile_count, weights, bias_vector):
    first_order = propagate(features, tile_values, tile_source, tile_target, tile_count).astype(jnp.bfloat16)
    second = propagate(first_order, tile_values, tile_source, tile_target, tile_count)
    second_order = (2.0 * second - features.astype(jnp.float32)).astype(jnp.bfloat16)
    result = jnp.dot(features, weights[0], preferred_element_type=jnp.float32)
    result = result + jnp.dot(first_order, weights[1], preferred_element_type=jnp.float32)
    result = result + jnp.dot(second_order, weights[2], preferred_element_type=jnp.float32)
    return (result + bias_vector[None, :]).astype(jnp.bfloat16)
```

```python
import functools

import jax
import jax.numpy as jnp
from jax import lax
from jax.experimental import pallas as pl
from jax.experimental.pallas import tpu as pltpu
from jax.sharding import PartitionSpec as P

MESH = pl.DeviceIdType.MESH
F32 = jnp.float32
BF16 = jnp.bfloat16
def fast_kernel(
    levels, f_any, tiles_any, src_any, tgt_any, w_any, bias_any, out_ref,
    f_ref, fall, fld1, fld2, tiles, sq, a_v, w_v, acc, base, fw1, inv, ints, tab_v, tab, bias_v,
    fsem, tsem, isem, psem, wsem, xs, xr, zs1, zr1, ys1, yr1, zs2, zr2, ys2, yr2,
):
    rt, tile = f_ref.shape[0], f_ref.shape[1]
    slots = tiles_any.shape[0]
    top = levels - 1
    me, mc = lax.axis_index("blk"), lax.axis_index("ch")
    z, y = lax.div(me, 2), lax.rem(me, 2)
    x, core = lax.div(mc, 2), lax.rem(mc, 2)
    partner = (me, 2 * x + (1 - core))
    across = (me, 2 * (1 - x) + core)
    y_dev = (2 * z + (1 - y), mc)
    z_dev = ((me + 2, mc), (me - 2, mc))
    can = (z < top, z > 0)

    barrier = pltpu.get_barrier_semaphore()
    for dev in (partner, across, y_dev):
        pl.semaphore_signal(barrier, inc=1, device_id=dev, device_id_type=MESH)
    for d in range(2):
        @pl.when(can[d])
        def _():
            pl.semaphore_signal(barrier, inc=1, device_id=z_dev[d], device_id_type=MESH)

    f_copy = pltpu.make_async_copy(f_any, f_ref, fsem)
    f_copy.start()
    int_copies = [
        pltpu.make_async_copy(src_any, ints.at[pl.ds(0, 1)], isem.at[0]),
        pltpu.make_async_copy(tgt_any, ints.at[pl.ds(1, 1)], isem.at[1]),
        pltpu.make_async_copy(bias_any, bias_v, isem.at[2]),
    ]
    for copy in int_copies:
        copy.start()
    tile_copy = pltpu.make_async_copy(tiles_any, tiles.at[pl.ds(0, slots)], tsem)
    tile_copy.start()
    order_of = (mc, partner[1], across[1], 2 * (1 - x) + (1 - core))

    def w_copy(s):
        q = pl.multiple_of(order_of[s] * tile, tile)
        p = pl.multiple_of(mc * tile, tile)
        return pltpu.make_async_copy(w_any.at[:, pl.ds(q, tile), pl.ds(p, tile)], w_v.at[s], wsem.at[s])

    for s in range(4):
        w_copy(s).start()

    tiles[slots] = jnp.zeros((tile, tile), BF16)
    sq[slots] = jnp.zeros((tile, tile), F32)

    for copy in int_copies:
        copy.wait()
    lane = lax.broadcasted_iota(jnp.int32, (slots, slots), 1)
    sub = lax.broadcasted_iota(jnp.int32, (slots, slots), 0)
    src_r, tgt_r = ints[0:1, :], ints[1:2, :]
    live = src_r < 2 * levels * rt
    key = jnp.broadcast_to(jnp.where(live, src_r * 8 + tgt_r, -1), (slots, slots))
    key_t = key.T
    target = jnp.broadcast_to(jnp.where(live, tgt_r, -1), (slots, slots))
    target_t = target.T

    def latest(hit):
        found = jnp.max(jnp.where(hit, sub, -1), axis=0, keepdims=True)
        return jnp.where(found < 0, slots, found)

    tab_v[0:1, :] = latest((key_t == key) & (sub < lane))
    tab_v[1:2, :] = latest((target_t == target) & (sub < lane))
    pair_rows = (2 * levels * rt * 8) // slots
    for i in range(pair_rows):
        tab_v[2 + i : 3 + i, :] = latest(key_t == lane + i * slots)
    tab_v[2 + pair_rows : 3 + pair_rows, :] = latest(target_t == lane)
    tab_copy = pltpu.make_async_copy(tab_v, tab, psem)
    tab_copy.start()
    f_copy.wait()

    pl.semaphore_wait(barrier, 3 + can[0].astype(jnp.int32) + can[1].astype(jnp.int32))

    def remote(src, dst, ssem, rsem, dev):
        return pltpu.make_async_remote_copy(
            src_ref=src, dst_ref=dst, send_sem=ssem, recv_sem=rsem, device_id=dev, device_id_type=MESH
        )

    order = [rt - 1] + list(range(rt - 1))

    def x_copy(kind, c):
        src = f_ref.at[c] if kind < 2 else fall.at[1, c]
        return remote(
            src, fall.at[kind, c], xs.at[kind], xr.at[kind, c], across if kind == 1 else partner
        )

    for c in order:
        x_copy(1, c).start()
        x_copy(0, c).start()

    tab_copy.wait()
    tile_copy.wait()

    def chain(k, _):
        value = tiles[k]
        wide = value.astype(F32)
        sq[k] = sq[tab[1, k]] + wide * wide
        tiles[k] = (wide + tiles[tab[0, k]].astype(F32)).astype(BF16)
        return 0

    lax.fori_loop(0, slots, chain, 0, unroll=2)

    def at(fld, block, it):
        return fld.at[block * rt + it]

    def z_view(fld, d, k, it):
        level = z - k if d == 0 else z + k
        return at(fld, 2 * level + y, it) if it < rt else at(fld, 2 * level + (1 - y), rt - 1)

    def z_copy(fld, zs, zr, d, k, it):
        view = z_view(fld, d, k, it)
        return remote(view, view, zs.at[d, k], zr.at[d, k, it], z_dev[d])

    def z_has(d, k):
        return z - k >= 0 if d == 0 else z + k <= top

    def y_index(d, k):
        return 0 if k == 0 else (1 + k - 1 if d == 0 else levels + k - 1)

    def y_sem(yr, d, k, it):
        return yr.at[y_index(d, k)] if it < rt - 1 else yr.at[2 * levels - 1]

    def y_copy(fld, ys, yr, d, k, it):
        level = z - k if d == 0 else z + k
        view = at(fld, 2 * level + y, it)
        return remote(view, view, ys, y_sem(yr, d, k, it), y_dev)

    def y_wait(fld, ys, yr, d, k):
        level = z - k if d == 0 else z + k
        view = fld.at[pl.ds((2 * level + (1 - y)) * rt, rt - 1)]
        remote(view, view, ys, yr.at[y_index(d, k)], y_dev).wait_recv()

    def multiply(fld, block, fetch, init=False):
        if fetch:
            for t in range(rt):
                for s in range(rt):
                    spot = (block * rt + s) * 8 + t
                    slot = tab[2 + lax.div(spot, slots), lax.rem(spot, slots)]
                    a_v[block, t * tile : (t + 1) * tile, s * tile : (s + 1) * tile] = tiles[slot]
        half = rt * tile // 2
        rhs = fld[pl.ds(block * rt, rt)].reshape(rt * tile, tile)

        @pl.loop(0, 2)
        def _(h):
            rows = pl.ds(pl.multiple_of(h * half, half), half)
            product = jnp.dot(a_v[block, rows, :], rhs, preferred_element_type=F32)
            acc[rows, :] = product if init else acc[rows, :] + product

    def emit_own(fld, sems, c):
        zs, zr, ys, yr = sems
        y_copy(fld, ys, yr, 0, 0, c).start()
        for d in range(2):
            @pl.when(can[d])
            def _():
                z_copy(fld, zs, zr, d, 0, c).start()

    def gather(fld, sems, fetch):
        zs, zr, ys, yr = sems
        view = at(fld, 2 * z + (1 - y), rt - 1)
        remote(view, view, ys, yr.at[2 * levels - 1], y_dev).wait_recv()
        for d in range(2):
            @pl.when(can[d])
            def _():
                z_copy(fld, zs, zr, d, 0, rt).start()
        multiply(fld, me, fetch, init=True)
        for k in range(1, levels):
            for it in order + [rt]:
                for d in range(2):
                    @pl.when(z_has(d, k))
                    def _():
                        remote(
                            z_view(fld, d, k, it), z_view(fld, d, k, it),
                            zs.at[d, k - 1], zr.at[d, k - 1, it], y_dev,
                        ).wait_recv()
                        if it < rt - 1:
                            y_copy(fld, ys, yr, d, k, it).start()
                        if k < top:
                            @pl.when(can[d])
                            def _():
                                z_copy(fld, zs, zr, d, k, it).start()
            if k == 1:
                y_wait(fld, ys, yr, 0, 0)
                multiply(fld, 2 * z + (1 - y), fetch)
            for d in range(2):
                @pl.when(z_has(d, k))
                def _():
                    level = z - k if d == 0 else z + k
                    multiply(fld, 2 * level + y, fetch)
                if k > 1:
                    other(fld, ys, yr, d, k - 1, fetch)
        for d in range(2):
            other(fld, ys, yr, d, top, fetch)

    def other(fld, ys, yr, d, k, fetch):
        @pl.when(z_has(d, k))
        def _():
            y_wait(fld, ys, yr, d, k)
            level = z - k if d == 0 else z + k
            multiply(fld, 2 * level + (1 - y), fetch)

    def drain(fld, sems):
        zs, zr, ys, yr = sems
        view = fld.at[pl.ds(0, rt + top * (rt - 1))]
        remote(view, view, ys, yr.at[0], y_dev).wait_send()
        view = fld.at[pl.ds(0, rt + 1)]
        for d in range(2):
            for k in range(top):
                @pl.when(z_has(d, k) & can[d])
                def _():
                    remote(view, view, zs.at[d, k], zr.at[d, k, 0], z_dev[d]).wait_send()

    sems1 = (zs1, zr1, ys1, yr1)
    sems2 = (zs2, zr2, ys2, yr2)
    bias = bias_v[:, pl.ds(pl.multiple_of(mc * tile, tile), tile)]
    for s in range(4):
        w_copy(s).wait()

    for c in order:
        x_copy(1, c).wait_recv()
        x_copy(2, c).start()
        x_copy(0, c).wait_recv()
        parts = (f_ref[c], fall[0, c], fall[1, c])
        r = [sum(jnp.dot(p, w_v[s, o], preferred_element_type=F32) for s, p in enumerate(parts)) for o in range(3)]
        x_copy(2, c).wait_recv()
        r = [r[o] + jnp.dot(fall[2, c], w_v[3, o], preferred_element_type=F32) for o in range(3)]
        fld1[me * rt + c] = r[2].astype(BF16)
        emit_own(fld1, sems1, c)
        rows = pl.ds(c * tile, tile)
        base[rows, :] = r[0] - r[2] + bias
        fw1[rows, :] = r[1]

    for t in range(rt):
        total = jnp.sum(sq[tab[2 + pair_rows, t]], axis=1, keepdims=True)
        inv[pl.ds(t * tile, tile), :] = jnp.broadcast_to(lax.rsqrt(1.0 + total), (tile, tile))

    gather(fld1, sems1, True)
    for c in order:
        rows = pl.ds(c * tile, tile)
        fld2[me * rt + c] = (fw1[rows, :] + 2.0 * (acc[rows, :] * inv[rows, :])).astype(BF16)
        emit_own(fld2, sems2, c)
    gather(fld2, sems2, False)
    out_ref[...] = (base[...] + acc[...] * inv[...]).astype(BF16)
    for kind in range(3):
        remote(f_ref, f_ref, xs.at[kind], xr.at[kind, 0], partner).wait_send()
    drain(fld1, sems1)
    drain(fld2, sems2)


def fast(features, tile_values, tile_source, tile_target, tile_count, weights, bias_vector):
    slots, tile, _ = tile_values.shape
    rows, cols = features.shape
    rt = rows // tile
    blocks = lax.axis_size("blk")
    levels = blocks // 2
    vmem = pl.BlockSpec(memory_space=pltpu.VMEM)
    hbm = pl.BlockSpec(memory_space=pltpu.HBM)
    dma = pltpu.SemaphoreType.DMA
    gather_sems = [
        dma((2, levels - 1)), dma((2, levels - 1, rt + 1)), dma, dma((2 * levels,)),
    ]
    return pl.pallas_call(
        functools.partial(fast_kernel, levels),
        out_shape=jax.ShapeDtypeStruct((rows, cols), BF16),
        in_specs=[hbm] * 6,
        out_specs=vmem,
        scratch_shapes=[
            pltpu.VMEM((rt, tile, tile), BF16),
            pltpu.VMEM((3, rt, tile, tile), BF16),
            pltpu.VMEM((blocks * rt, tile, tile), BF16),
            pltpu.VMEM((blocks * rt, tile, tile), BF16),
            pltpu.VMEM((slots + 1, tile, tile), BF16),
            pltpu.VMEM((slots + 1, tile, tile), F32),
            pltpu.VMEM((blocks, rows, rows), BF16),
            pltpu.VMEM((4, 3, tile, tile), BF16),
            pltpu.VMEM((rows, tile), F32),
            pltpu.VMEM((rows, tile), F32),
            pltpu.VMEM((rows, tile), F32),
            pltpu.VMEM((rows, tile), F32),
            pltpu.VMEM((8, tile), jnp.int32),
            pltpu.VMEM((8, slots), jnp.int32),
            pltpu.SMEM((8, slots), jnp.int32),
            pltpu.VMEM((1, 4 * cols), F32),
            dma, dma, dma((3,)), dma, dma((4,)), dma((3,)), dma((3, rt)),
        ] + gather_sems + gather_sems,
        compiler_params=pltpu.CompilerParams(collective_id=0, has_side_effects=True, vmem_limit_bytes=58 << 20),
        name="propagate",
    )(
        features.reshape(rt, tile, cols), tile_values, tile_source.reshape(1, -1), tile_target.reshape(1, -1),
        weights, bias_vector.reshape(1, -1),
    )


def per_device(features, tile_values, tile_source, tile_target, tile_count, weights, bias_vector):
    tile_size = tile_values.shape[1]
    slot_total = tile_values.shape[0]
    channels = features.shape[1]
    row_tiles = features.shape[0] // tile_size
    block_rows = row_tiles * tile_size
    block_count = lax.axis_size("blk")
    slot_cap = max(2, (2 * slot_total + block_count - 1) // block_count)
    usable = jnp.arange(slot_total, dtype=jnp.int32) < tile_count[0]
    squares = jnp.einsum(
        "tij,tij->ti", tile_values, tile_values, preferred_element_type=jnp.float32
    )
    squares = jnp.where(usable[:, None], squares, 0.0)
    onehot = (
        (tile_target[:, None] == jnp.arange(row_tiles, dtype=jnp.int32)[None, :]) & usable[:, None]
    ).astype(jnp.float32)
    row_norm = jnp.dot(onehot.T, squares, precision=lax.Precision.HIGHEST)
    inverse = lax.rsqrt(1.0 + row_norm).reshape(-1)
    zero_sum = jnp.zeros((row_tiles, tile_size, channels), jnp.float32)

    def cycle_prop(signal):
        segment = lax.all_gather(signal, "blk", axis=0, tiled=True)
        offset = jnp.int32(0)
        count_rows = segment.shape[0]
        window = min(slot_total, slot_cap * (count_rows // block_rows + 2))
        low_row = tile_source * tile_size
        first_slot = jnp.sum(usable & (low_row + tile_size <= offset))
        end_slot = jnp.sum(usable & (low_row < offset + count_rows))
        start_slot = jnp.minimum(first_slot, slot_total - window)
        slot_ids = start_slot + jnp.arange(window, dtype=jnp.int32)
        in_range = (slot_ids >= first_slot) & (slot_ids < end_slot)
        row_ids = tile_source[:, None] * tile_size + jnp.arange(tile_size, dtype=jnp.int32)[None, :]
        inside = (row_ids >= 0) & (row_ids < count_rows) & in_range[:, None]
        picked = jnp.take(segment, jnp.clip(row_ids, 0, count_rows - 1).reshape(-1), axis=0)
        picked = picked.reshape(window, tile_size, channels)
        picked = jnp.where(inside[:, :, None], picked, jnp.zeros((), segment.dtype))
        product = jnp.einsum(
            "gij,gjc->gic", tile_values, picked, preferred_element_type=jnp.float32
        )
        product = jnp.where(in_range[:, None, None], product, 0.0)
        summed = zero_sum.at[tile_target].add(product)
        return summed.reshape(-1, channels) * inverse[:, None]

    col_start = lax.axis_index("ch") * channels
    bias_part = lax.dynamic_slice_in_dim(bias_vector, col_start, channels, 0)
    w_cols = lax.dynamic_slice_in_dim(weights, col_start, channels, 2)

    def mix_term(order_term, order_index, running):
        w_slice = w_cols[order_index]
        return running + jnp.dot(
            lax.all_gather(order_term, "ch", axis=1, tiled=True),
            w_slice,
            preferred_element_type=jnp.float32,
        )

    result = mix_term(features, 0, jnp.zeros((features.shape[0], channels), jnp.float32))
    first_order = cycle_prop(features).astype(jnp.bfloat16)
    result = mix_term(first_order, 1, result)
    second_order = (2.0 * cycle_prop(first_order) - features.astype(jnp.float32)).astype(
        jnp.bfloat16
    )
    result = mix_term(second_order, 2, result)
    return (result + bias_part[None, :]).astype(jnp.bfloat16)


def solution(mesh):
    dense = mesh.shape["blk"] == 8 and mesh.shape["ch"] == 4
    return jax.shard_map(
        fast if dense else per_device,
        mesh=mesh,
        in_specs=(P("blk", "ch"), P("blk", None, None), P("blk"), P("blk"), P("blk"), P(), P()),
        out_specs=P("blk", "ch"),
        check_vma=False,
    )
```

```python
import functools

import jax
import jax.numpy as jnp
from jax import lax
from jax.experimental import pallas as pl
from jax.experimental.pallas import tpu as pltpu
from jax.sharding import PartitionSpec as P

MESH = pl.DeviceIdType.MESH
F32 = jnp.float32
BF16 = jnp.bfloat16
def fast_kernel(
    levels, f_any, tiles_any, src_any, tgt_any, w_any, bias_any, out_ref,
    f_ref, fall, main1, last1, main2, last2, tiles, sq, a_v, w_v, acc, base, fw1, inv, ints, tab_v, tab, bias_v,
    fsem, tsem, isem, psem, wsem, xs, xr, zs1, zr1, ys1, yr1, zs2, zr2, ys2, yr2,
):
    rt, tile = f_ref.shape[0], f_ref.shape[1]
    bulk = rt - 1
    slots = tiles_any.shape[0]
    top = levels - 1
    me, mc = lax.axis_index("blk"), lax.axis_index("ch")
    z, y = lax.div(me, 2), lax.rem(me, 2)
    x, core = lax.div(mc, 2), lax.rem(mc, 2)
    partner = (me, 2 * x + (1 - core))
    across = (me, 2 * (1 - x) + core)
    diagonal = (me, 2 * (1 - x) + (1 - core))
    y_dev = (2 * z + (1 - y), mc)
    z_dev = ((me + 2, mc), (me - 2, mc))
    can = (z < top, z > 0)

    barrier = pltpu.get_barrier_semaphore()
    for dev in (partner, across, diagonal, y_dev):
        pl.semaphore_signal(barrier, inc=1, device_id=dev, device_id_type=MESH)
    for d in range(2):
        @pl.when(can[d])
        def _():
            pl.semaphore_signal(barrier, inc=1, device_id=z_dev[d], device_id_type=MESH)

    f_copy = pltpu.make_async_copy(f_any, f_ref, fsem)
    f_copy.start()
    int_copies = [
        pltpu.make_async_copy(src_any, ints.at[pl.ds(0, 1)], isem.at[0]),
        pltpu.make_async_copy(tgt_any, ints.at[pl.ds(1, 1)], isem.at[1]),
        pltpu.make_async_copy(bias_any, bias_v, isem.at[2]),
    ]
    for copy in int_copies:
        copy.start()
    tile_copy = pltpu.make_async_copy(tiles_any, tiles.at[pl.ds(0, slots)], tsem)
    tile_copy.start()
    order_of = (mc, partner[1], across[1], 2 * (1 - x) + (1 - core))

    def w_copy(s):
        q = pl.multiple_of(order_of[s] * tile, tile)
        p = pl.multiple_of(mc * tile, tile)
        return pltpu.make_async_copy(w_any.at[:, pl.ds(q, tile), pl.ds(p, tile)], w_v.at[:, s], wsem.at[s])

    for s in range(4):
        w_copy(s).start()

    tiles[slots] = jnp.zeros((tile, tile), BF16)
    sq[slots] = jnp.zeros((tile, tile), F32)

    for copy in int_copies:
        copy.wait()
    lane = lax.broadcasted_iota(jnp.int32, (slots, slots), 1)
    sub = lax.broadcasted_iota(jnp.int32, (slots, slots), 0)
    src_r, tgt_r = ints[0:1, :], ints[1:2, :]
    live = src_r < 2 * levels * rt
    key = jnp.broadcast_to(jnp.where(live, src_r * 8 + tgt_r, -1), (slots, slots))
    key_t = key.T
    target = jnp.broadcast_to(jnp.where(live, tgt_r, -1), (slots, slots))
    target_t = target.T

    def latest(hit):
        found = jnp.max(jnp.where(hit, sub, -1), axis=0, keepdims=True)
        return jnp.where(found < 0, slots, found)

    tab_v[0:1, :] = latest((key_t == key) & (sub < lane))
    tab_v[1:2, :] = latest((target_t == target) & (sub < lane))
    pair_rows = (2 * levels * rt * 8) // slots
    for i in range(pair_rows):
        tab_v[2 + i : 3 + i, :] = latest(key_t == lane + i * slots)
    tab_v[2 + pair_rows : 3 + pair_rows, :] = latest(target_t == lane)
    tab_copy = pltpu.make_async_copy(tab_v, tab, psem)
    tab_copy.start()
    f_copy.wait()

    pl.semaphore_wait(barrier, 4 + can[0].astype(jnp.int32) + can[1].astype(jnp.int32))

    def remote(src, dst, ssem, rsem, dev):
        return pltpu.make_async_remote_copy(
            src_ref=src, dst_ref=dst, send_sem=ssem, recv_sem=rsem, device_id=dev, device_id_type=MESH
        )

    def x_copy(kind, c):
        if kind == 2 and c in direct:
            return remote(f_ref.at[c], fall.at[2, c], xs.at[2], xr.at[2, c], diagonal)
        src = f_ref.at[c] if kind < 2 else fall.at[1, c]
        return remote(
            src, fall.at[kind, c], xs.at[kind], xr.at[kind, c], across if kind == 1 else partner
        )

    order = [0, rt - 1] + list(range(1, rt - 1))
    direct = order[:6]
    for c in order:
        if c in direct:
            x_copy(2, c).start()
        x_copy(1, c).start()
        x_copy(0, c).start()

    tab_copy.wait()
    tile_copy.wait()

    def chain(k, _):
        value = tiles[k]
        wide = value.astype(F32)
        sq[k] = sq[tab[1, k]] + wide * wide
        tiles[k] = (wide + tiles[tab[0, k]].astype(F32)).astype(BF16)
        return 0

    lax.fori_loop(0, slots, chain, 0, unroll=2)

    def at(fld, block, it):
        return fld[0].at[block * bulk + it] if it < bulk else fld[1].at[block]

    def level_of(d, k):
        return z - k if d == 0 else z + k

    def shard(z0, d, k):
        return 2 * level_of(d, k)

    def z_view(fld, d, k, it):
        pair = shard(z, d, k)
        return at(fld, pair + y, it) if it < bulk else fld[1].at[pl.ds(pair, 2)]

    def z_copy(fld, sems, d, k, it):
        view = z_view(fld, d, k, it)
        level = level_of(d, k)
        return remote(view, view, z_sent(sems, d, k), sems[1].at[level, it], z_dev[d])

    def z_wait(fld, sems, d, k, it):
        view = z_view(fld, d, k, it)
        remote(view, view, sems[0].at[0], sems[1].at[level_of(d, k), it], y_dev).wait_recv()

    def z_has(d, k):
        return z - k >= 0 if d == 0 else z + k <= top

    def z_sent(sems, d, k):
        return sems[0].at[level_of(d, k) if k or d else levels]

    def y_copy(fld, sems, d, k, it):
        view = at(fld, shard(z, d, k) + y, it)
        sem = level_of(d, k) if it < bulk else levels
        return remote(view, view, sems[2], sems[3].at[sem], y_dev)

    def y_wait(fld, sems, d, k, last=False):
        other = shard(z, d, k) + (1 - y)
        view = fld[1].at[other] if last else fld[0].at[pl.ds(other * bulk, bulk)]
        sem = levels if last else level_of(d, k)
        remote(view, view, sems[2], sems[3].at[sem], y_dev).wait_recv()

    def fetch_block(block):
        for t in range(rt):
            for s in range(rt):
                spot = (block * rt + s) * 8 + t
                slot = tab[2 + lax.div(spot, slots), lax.rem(spot, slots)]
                a_v[block, t * tile : (t + 1) * tile, s * tile : (s + 1) * tile] = tiles[slot]

    def add(h, lhs, rhs, init):
        product = jnp.dot(lhs, rhs, preferred_element_type=F32)
        rows = slice(h * half, (h + 1) * half)
        acc[rows, :] = product if init else acc[rows, :] + product

    def bulk_half(fld, block, h, init=False):
        rhs = fld[0][pl.ds(block * bulk, bulk)].reshape(bulk * tile, tile)
        add(h, a_v[block, h * half : (h + 1) * half, : bulk * tile], rhs, init)

    def tail_half(fld, pair, h):
        lhs = [a_v[pair + i, h * half : (h + 1) * half, bulk * tile :] for i in range(2)]
        rhs = fld[1][pl.ds(pair, 2)].reshape(2 * tile, tile)
        add(h, jnp.concatenate(lhs, axis=1), rhs, False)

    def bulk_work(fld, block, fetch, init=False):
        first = [lambda: fetch_block(block)] if fetch else []
        return first + [lambda h=h: bulk_half(fld, block, h, init) for h in range(2)]

    def tail_work(fld, pair):
        return [lambda h=h: tail_half(fld, pair, h) for h in range(2)]

    def emit_own(fld, sems, c):
        y_copy(fld, sems, 0, 0, c).start()
        if c < bulk:
            for d in range(2):
                @pl.when(can[d])
                def _():
                    z_copy(fld, sems, d, 0, c).start()

    def gather(fld, sems, extra, late):
        fetch = False
        todo = bulk_work(fld, me, fetch, True) + extra

        def step():
            if todo:
                todo.pop(0)()

        def when_has(d, k, work):
            def go(w):
                @pl.when(z_has(d, k))
                def _():
                    w()
            todo.extend([functools.partial(go, w) for w in work])

        def finish():
            while todo:
                step()

        def own_tail(d, ready):
            @pl.when(can[d] & ready)
            def _():
                z_copy(fld, sems, d, 0, bulk).start()

        def tail(d, k):
            @pl.when(z_has(d, k))
            def _():
                z_wait(fld, sems, d, k, bulk)
                if k < top:
                    @pl.when(can[d])
                    def _():
                        z_copy(fld, sems, d, k, bulk).start()
            when_has(d, k, tail_work(fld, shard(z, d, k)))

        def others(d, k, when):
            @pl.when(when)
            def _():
                y_wait(fld, sems, d, k)
                for w in bulk_work(fld, shard(z, d, k) + (1 - y), fetch):
                    w()

        ends = (z, top - z)
        for k in range(1, levels):
            for it in range(bulk):
                step()
                for d in range(2):
                    @pl.when(z_has(d, k))
                    def _():
                        z_wait(fld, sems, d, k, it)
                        y_copy(fld, sems, d, k, it).start()
                        if k < top:
                            @pl.when(can[d])
                            def _():
                                z_copy(fld, sems, d, k, it).start()
                if k == 1 and it == 1:
                    y_wait(fld, sems, 0, 0, True)
                    for d in range(2):
                        own_tail(d, ends[d] == 0 if late else True)
            for d in range(2):
                if late:
                    own_tail(d, ends[d] == k)
                else:
                    tail(d, k)
            finish()
            if k == 1:
                y_wait(fld, sems, 0, 0)
                todo.extend(bulk_work(fld, shard(z, 0, 0) + (1 - y), fetch))
                todo.extend(tail_work(fld, shard(z, 0, 0)))
            for d in range(2):
                when_has(d, k, bulk_work(fld, shard(z, d, k) + y, fetch))
                if k > 1 and not late:
                    others(d, k - 1, z_has(d, k - 1))
        finish()
        if late:
            corner = (z_has(0, top), z_has(1, top))
            for k in range(1, levels):
                for d in range(2):
                    if k < top:
                        others(d, k, corner[d])
                for d in range(2):
                    tail(d, k)
                if k == top - 1:
                    finish()
            finish()
            for k in range(1, top):
                for d in range(2):
                    others(d, k, z_has(d, k) & jnp.logical_not(corner[d]))
        for d in range(2):
            others(d, top, z_has(d, top))
        finish()

    def drain(fld, sems):
        view = fld[0].at[pl.ds(0, rt + top * bulk)]
        remote(view, view, sems[2], sems[3].at[0], y_dev).wait_send()
        view = fld[0].at[pl.ds(0, bulk + 2)]
        for d in range(2):
            for k in range(top):
                @pl.when(z_has(d, k) & can[d])
                def _():
                    remote(view, view, z_sent(sems, d, k), sems[1].at[0, 0], z_dev[d]).wait_send()

    half = rt * tile // 2
    fld1, fld2 = (main1, last1), (main2, last2)
    sems1 = (zs1, zr1, ys1, yr1)
    sems2 = (zs2, zr2, ys2, yr2)
    bias = bias_v[:, pl.ds(pl.multiple_of(mc * tile, tile), tile)]
    for s in range(4):
        w_copy(s).wait()

    def mixed_rows(c):
        return jnp.concatenate([f_ref[c], fall[0, c], fall[1, c], fall[2, c]], axis=1)

    def mix(c):
        both = jnp.concatenate([w_v[o].reshape(4 * tile, tile) for o in range(2)], axis=1)
        r = jnp.dot(mixed_rows(c), both, preferred_element_type=F32)
        rows = pl.ds(c * tile, tile)
        base[rows, :] = base[rows, :] + r[:, :tile]
        fw1[rows, :] = r[:, tile:]

    blocks_left = list(range(2 * levels))
    for _ in range(2):
        fetch_block(blocks_left.pop(0))
    for c in order:
        x_copy(1, c).wait_recv()
        if c not in direct:
            x_copy(2, c).start()
        x_copy(0, c).wait_recv()
        x_copy(2, c).wait_recv()
        r = jnp.dot(mixed_rows(c), w_v[2].reshape(4 * tile, tile), preferred_element_type=F32)
        at(fld1, me, c)[...] = r.astype(BF16)
        emit_own(fld1, sems1, c)
        rows = pl.ds(c * tile, tile)
        base[rows, :] = bias - r
        if blocks_left:
            fetch_block(blocks_left.pop(0))

    for t in range(rt):
        total = jnp.sum(sq[tab[2 + pair_rows, t]], axis=1, keepdims=True)
        inv[pl.ds(t * tile, tile), :] = jnp.broadcast_to(lax.rsqrt(1.0 + total), (tile, tile))

    for block in blocks_left:
        fetch_block(block)
    gather(fld1, sems1, [functools.partial(mix, c) for c in range(rt)], True)
    for c in order:
        rows = pl.ds(c * tile, tile)
        at(fld2, me, c)[...] = (fw1[rows, :] + 2.0 * (acc[rows, :] * inv[rows, :])).astype(BF16)
        emit_own(fld2, sems2, c)
    gather(fld2, sems2, [], True)
    out_ref[...] = (base[...] + acc[...] * inv[...]).astype(BF16)
    for kind in range(3):
        remote(f_ref, f_ref, xs.at[kind], xr.at[kind, 0], partner).wait_send()
    drain(fld1, sems1)
    drain(fld2, sems2)


def fast(features, tile_values, tile_source, tile_target, tile_count, weights, bias_vector):
    slots, tile, _ = tile_values.shape
    rows, cols = features.shape
    rt = rows // tile
    blocks = lax.axis_size("blk")
    levels = blocks // 2
    vmem = pl.BlockSpec(memory_space=pltpu.VMEM)
    hbm = pl.BlockSpec(memory_space=pltpu.HBM)
    dma = pltpu.SemaphoreType.DMA
    gather_sems = [
        dma((levels + 1,)), dma((levels, rt)), dma, dma((levels + 1,)),
    ]
    return pl.pallas_call(
        functools.partial(fast_kernel, levels),
        out_shape=jax.ShapeDtypeStruct((rows, cols), BF16),
        in_specs=[hbm] * 6,
        out_specs=vmem,
        scratch_shapes=[
            pltpu.VMEM((rt, tile, tile), BF16),
            pltpu.VMEM((3, rt, tile, tile), BF16),
            pltpu.VMEM((blocks * (rt - 1), tile, tile), BF16),
            pltpu.VMEM((blocks, tile, tile), BF16),
            pltpu.VMEM((blocks * (rt - 1), tile, tile), BF16),
            pltpu.VMEM((blocks, tile, tile), BF16),
            pltpu.VMEM((slots + 1, tile, tile), BF16),
            pltpu.VMEM((slots + 1, tile, tile), F32),
            pltpu.VMEM((blocks, rows, rows), BF16),
            pltpu.VMEM((3, 4, tile, tile), BF16),
            pltpu.VMEM((rows, tile), F32),
            pltpu.VMEM((rows, tile), F32),
            pltpu.VMEM((rows, tile), F32),
            pltpu.VMEM((rows, tile), F32),
            pltpu.VMEM((8, tile), jnp.int32),
            pltpu.VMEM((8, slots), jnp.int32),
            pltpu.SMEM((8, slots), jnp.int32),
            pltpu.VMEM((1, 4 * cols), F32),
            dma, dma, dma((3,)), dma, dma((4,)), dma((3,)), dma((3, rt)),
        ] + gather_sems + gather_sems,
        compiler_params=pltpu.CompilerParams(collective_id=0, has_side_effects=True, vmem_limit_bytes=58 << 20),
        name="propagate",
    )(
        features.reshape(rt, tile, cols), tile_values, tile_source.reshape(1, -1), tile_target.reshape(1, -1),
        weights, bias_vector.reshape(1, -1),
    )


def per_device(features, tile_values, tile_source, tile_target, tile_count, weights, bias_vector):
    tile_size = tile_values.shape[1]
    slot_total = tile_values.shape[0]
    channels = features.shape[1]
    row_tiles = features.shape[0] // tile_size
    block_rows = row_tiles * tile_size
    block_count = lax.axis_size("blk")
    slot_cap = max(2, (2 * slot_total + block_count - 1) // block_count)
    usable = jnp.arange(slot_total, dtype=jnp.int32) < tile_count[0]
    squares = jnp.einsum(
        "tij,tij->ti", tile_values, tile_values, preferred_element_type=jnp.float32
    )
    squares = jnp.where(usable[:, None], squares, 0.0)
    onehot = (
        (tile_target[:, None] == jnp.arange(row_tiles, dtype=jnp.int32)[None, :]) & usable[:, None]
    ).astype(jnp.float32)
    row_norm = jnp.dot(onehot.T, squares, precision=lax.Precision.HIGHEST)
    inverse = lax.rsqrt(1.0 + row_norm).reshape(-1)
    zero_sum = jnp.zeros((row_tiles, tile_size, channels), jnp.float32)

    def cycle_prop(signal):
        segment = lax.all_gather(signal, "blk", axis=0, tiled=True)
        offset = jnp.int32(0)
        count_rows = segment.shape[0]
        window = min(slot_total, slot_cap * (count_rows // block_rows + 2))
        low_row = tile_source * tile_size
        first_slot = jnp.sum(usable & (low_row + tile_size <= offset))
        end_slot = jnp.sum(usable & (low_row < offset + count_rows))
        start_slot = jnp.minimum(first_slot, slot_total - window)
        slot_ids = start_slot + jnp.arange(window, dtype=jnp.int32)
        in_range = (slot_ids >= first_slot) & (slot_ids < end_slot)
        row_ids = tile_source[:, None] * tile_size + jnp.arange(tile_size, dtype=jnp.int32)[None, :]
        inside = (row_ids >= 0) & (row_ids < count_rows) & in_range[:, None]
        picked = jnp.take(segment, jnp.clip(row_ids, 0, count_rows - 1).reshape(-1), axis=0)
        picked = picked.reshape(window, tile_size, channels)
        picked = jnp.where(inside[:, :, None], picked, jnp.zeros((), segment.dtype))
        product = jnp.einsum(
            "gij,gjc->gic", tile_values, picked, preferred_element_type=jnp.float32
        )
        product = jnp.where(in_range[:, None, None], product, 0.0)
        summed = zero_sum.at[tile_target].add(product)
        return summed.reshape(-1, channels) * inverse[:, None]

    col_start = lax.axis_index("ch") * channels
    bias_part = lax.dynamic_slice_in_dim(bias_vector, col_start, channels, 0)
    w_cols = lax.dynamic_slice_in_dim(weights, col_start, channels, 2)

    def mix_term(order_term, order_index, running):
        w_slice = w_cols[order_index]
        return running + jnp.dot(
            lax.all_gather(order_term, "ch", axis=1, tiled=True),
            w_slice,
            preferred_element_type=jnp.float32,
        )

    result = mix_term(features, 0, jnp.zeros((features.shape[0], channels), jnp.float32))
    first_order = cycle_prop(features).astype(jnp.bfloat16)
    result = mix_term(first_order, 1, result)
    second_order = (2.0 * cycle_prop(first_order) - features.astype(jnp.float32)).astype(
        jnp.bfloat16
    )
    result = mix_term(second_order, 2, result)
    return (result + bias_part[None, :]).astype(jnp.bfloat16)


def solution(mesh):
    dense = mesh.shape["blk"] == 8 and mesh.shape["ch"] == 4
    return jax.shard_map(
        fast if dense else per_device,
        mesh=mesh,
        in_specs=(P("blk", "ch"), P("blk", None, None), P("blk"), P("blk"), P("blk"), P(), P()),
        out_specs=P("blk", "ch"),
        check_vma=False,
    )
```

```python
import functools

import jax
import jax.numpy as jnp
from jax import lax
from jax.experimental import pallas as pl
from jax.experimental.pallas import tpu as pltpu
from jax.sharding import PartitionSpec as P

MESH = pl.DeviceIdType.MESH
F32 = jnp.float32
BF16 = jnp.bfloat16
def fast_kernel(
    levels, f_any, tiles_any, src_any, tgt_any, w_any, bias_any, out_ref,
    f_ref, fall, main1, last1, main2, last2, tiles, sq, a_v, w_v, acc, base, fw1, inv, ints, tab_v, tab, bias_v,
    fsem, tsem, isem, psem, wsem, xs, xr, zs1, zr1, ys1, yr1, zs2, zr2, ys2, yr2,
):
    rt, tile = f_ref.shape[0], f_ref.shape[1]
    bulk = rt - 1
    slots = tiles_any.shape[0]
    top = levels - 1
    me, mc = lax.axis_index("blk"), lax.axis_index("ch")
    z, y = lax.div(me, 2), lax.rem(me, 2)
    x, core = lax.div(mc, 2), lax.rem(mc, 2)
    partner = (me, 2 * x + (1 - core))
    across = (me, 2 * (1 - x) + core)
    y_dev = (2 * z + (1 - y), mc)
    z_dev = ((me + 2, mc), (me - 2, mc))
    can = (z < top, z > 0)

    barrier = pltpu.get_barrier_semaphore()
    for dev in (partner, across, y_dev):
        pl.semaphore_signal(barrier, inc=1, device_id=dev, device_id_type=MESH)
    for d in range(2):
        @pl.when(can[d])
        def _():
            pl.semaphore_signal(barrier, inc=1, device_id=z_dev[d], device_id_type=MESH)

    f_copy = pltpu.make_async_copy(f_any, f_ref, fsem)
    f_copy.start()
    int_copies = [
        pltpu.make_async_copy(src_any, ints.at[pl.ds(0, 1)], isem.at[0]),
        pltpu.make_async_copy(tgt_any, ints.at[pl.ds(1, 1)], isem.at[1]),
        pltpu.make_async_copy(bias_any, bias_v, isem.at[2]),
    ]
    for copy in int_copies:
        copy.start()
    tile_copy = pltpu.make_async_copy(tiles_any, tiles.at[pl.ds(0, slots)], tsem)
    tile_copy.start()
    order_of = (mc, partner[1], across[1], 2 * (1 - x) + (1 - core))

    def w_copy(s):
        q = pl.multiple_of(order_of[s] * tile, tile)
        p = pl.multiple_of(mc * tile, tile)
        return pltpu.make_async_copy(w_any.at[:, pl.ds(q, tile), pl.ds(p, tile)], w_v.at[:, s], wsem.at[s])

    for s in range(4):
        w_copy(s).start()

    tiles[slots] = jnp.zeros((tile, tile), BF16)
    sq[slots] = jnp.zeros((tile, tile), F32)

    for copy in int_copies:
        copy.wait()
    lane = lax.broadcasted_iota(jnp.int32, (slots, slots), 1)
    sub = lax.broadcasted_iota(jnp.int32, (slots, slots), 0)
    src_r, tgt_r = ints[0:1, :], ints[1:2, :]
    live = src_r < 2 * levels * rt
    key = jnp.broadcast_to(jnp.where(live, src_r * 8 + tgt_r, -1), (slots, slots))
    key_t = key.T
    target = jnp.broadcast_to(jnp.where(live, tgt_r, -1), (slots, slots))
    target_t = target.T

    def latest(hit):
        found = jnp.max(jnp.where(hit, sub, -1), axis=0, keepdims=True)
        return jnp.where(found < 0, slots, found)

    tab_v[0:1, :] = latest((key_t == key) & (sub < lane))
    tab_v[1:2, :] = latest((target_t == target) & (sub < lane))
    pair_rows = (2 * levels * rt * 8) // slots
    for i in range(pair_rows):
        tab_v[2 + i : 3 + i, :] = latest(key_t == lane + i * slots)
    tab_v[2 + pair_rows : 3 + pair_rows, :] = latest(target_t == lane)
    tab_copy = pltpu.make_async_copy(tab_v, tab, psem)
    tab_copy.start()
    f_copy.wait()

    pl.semaphore_wait(barrier, 3 + can[0].astype(jnp.int32) + can[1].astype(jnp.int32))

    def remote(src, dst, ssem, rsem, dev):
        return pltpu.make_async_remote_copy(
            src_ref=src, dst_ref=dst, send_sem=ssem, recv_sem=rsem, device_id=dev, device_id_type=MESH
        )

    def x_copy(kind, c):
        src = f_ref.at[c] if kind < 2 else fall.at[1, c]
        return remote(
            src, fall.at[kind, c], xs.at[kind], xr.at[kind, c], across if kind == 1 else partner
        )

    order = [0, rt - 1] + list(range(1, rt - 1))
    for c in order:
        x_copy(1, c).start()
        x_copy(0, c).start()

    tab_copy.wait()
    tile_copy.wait()

    def chain(k, _):
        value = tiles[k]
        wide = value.astype(F32)
        sq[k] = sq[tab[1, k]] + wide * wide
        tiles[k] = (wide + tiles[tab[0, k]].astype(F32)).astype(BF16)
        return 0

    lax.fori_loop(0, slots, chain, 0, unroll=2)

    def at(fld, block, it):
        return fld[0].at[block * bulk + it] if it < bulk else fld[1].at[block]

    def level_of(d, k):
        return z - k if d == 0 else z + k

    def shard(z0, d, k):
        return 2 * level_of(d, k)

    def z_view(fld, d, k, it):
        pair = shard(z, d, k)
        return at(fld, pair + y, it) if it < bulk else fld[1].at[pl.ds(pair, 2)]

    def z_copy(fld, sems, d, k, it):
        view = z_view(fld, d, k, it)
        level = level_of(d, k)
        return remote(view, view, z_sent(sems, d, k), sems[1].at[level, it], z_dev[d])

    def side_copy(fld, sems, d, count):
        view = fld[0].at[pl.ds((shard(z, 0, 0) + (1 - y)) * bulk, count)]
        return remote(view, view, z_sent(sems, d, 0), sems[3].at[z], z_dev[d])

    def z_wait(fld, sems, d, k, it):
        view = z_view(fld, d, k, it)
        remote(view, view, sems[0].at[0], sems[1].at[level_of(d, k), it], y_dev).wait_recv()

    def z_has(d, k):
        return z - k >= 0 if d == 0 else z + k <= top

    def z_sent(sems, d, k):
        return sems[0].at[level_of(d, k) if k or d else levels]

    def y_copy(fld, sems, d, k, it):
        view = at(fld, shard(z, d, k) + y, it)
        sem = level_of(d, k) if it < bulk else levels
        return remote(view, view, sems[2], sems[3].at[sem], y_dev)

    def y_wait(fld, sems, d, k, last=False):
        other = shard(z, d, k) + (1 - y)
        view = fld[1].at[other] if last else fld[0].at[pl.ds(other * bulk, bulk)]
        sem = levels if last else level_of(d, k)
        remote(view, view, sems[2], sems[3].at[sem], y_dev).wait_recv()

    def fetch_block(block):
        for t in range(rt):
            for s in range(rt):
                spot = (block * rt + s) * 8 + t
                slot = tab[2 + lax.div(spot, slots), lax.rem(spot, slots)]
                a_v[block, t * tile : (t + 1) * tile, s * tile : (s + 1) * tile] = tiles[slot]

    def add(h, lhs, rhs, init):
        product = jnp.dot(lhs, rhs, preferred_element_type=F32)
        rows = slice(h * half, (h + 1) * half)
        acc[rows, :] = product if init else acc[rows, :] + product

    def bulk_half(fld, block, h, init=False):
        rhs = fld[0][pl.ds(block * bulk, bulk)].reshape(bulk * tile, tile)
        add(h, a_v[block, h * half : (h + 1) * half, : bulk * tile], rhs, init)

    def tail_half(fld, pair, h):
        lhs = [a_v[pair + i, h * half : (h + 1) * half, bulk * tile :] for i in range(2)]
        rhs = fld[1][pl.ds(pair, 2)].reshape(2 * tile, tile)
        add(h, jnp.concatenate(lhs, axis=1), rhs, False)

    def bulk_work(fld, block, fetch, init=False):
        first = [lambda: fetch_block(block)] if fetch else []
        return first + [lambda h=h: bulk_half(fld, block, h, init) for h in range(2)]

    def tail_work(fld, pair):
        return [lambda h=h: tail_half(fld, pair, h) for h in range(2)]

    def emit_own(fld, sems, c):
        y_copy(fld, sems, 0, 0, c).start()
        if c < bulk:
            for d in range(2):
                @pl.when(can[d])
                def _():
                    z_copy(fld, sems, d, 0, c).start()

    corner = (z == top, z == 0)
    near = (z == 1, z == top - 1)

    def gather(fld, sems, extra, late, asym, shift):
        fetch = False
        todo = bulk_work(fld, me, fetch, True) + extra

        def step():
            if todo:
                todo.pop(0)()

        def when_has(d, k, work):
            def go(w):
                @pl.when(z_has(d, k))
                def _():
                    w()
            todo.extend([functools.partial(go, w) for w in work])

        def finish():
            while todo:
                step()

        def own_tail(d, ready):
            @pl.when(can[d] & ready)
            def _():
                z_copy(fld, sems, d, 0, bulk).start()

        def tail(d, k):
            @pl.when(z_has(d, k))
            def _():
                z_wait(fld, sems, d, k, bulk)
                if k < top:
                    @pl.when(can[d])
                    def _():
                        z_copy(fld, sems, d, k, bulk).start()
            when_has(d, k, tail_work(fld, shard(z, d, k)))

        def others(d, k, when):
            @pl.when(when)
            def _():
                y_wait(fld, sems, d, k)
                for w in bulk_work(fld, shard(z, d, k) + (1 - y), fetch):
                    w()

        ends = (z, top - z)
        for k in range(1, levels):
            for it in range(bulk):
                step()
                for d in range(2):
                    @pl.when(z_has(d, k))
                    def _():
                        z_wait(fld, sems, d, k, it)
                        if k == 1:
                            skip = near[d] if asym else z < 0
                            if it < shift:
                                skip = skip | corner[d]

                            @pl.when(jnp.logical_not(skip))
                            def _():
                                y_copy(fld, sems, d, k, it).start()
                        else:
                            y_copy(fld, sems, d, k, it).start()
                        if k < top:
                            @pl.when(can[d])
                            def _():
                                z_copy(fld, sems, d, k, it).start()
                if k == 1 and it == 1:
                    y_wait(fld, sems, 0, 0, True)
                    for d in range(2):
                        own_tail(d, ends[d] == 0 if late else True)
            for d in range(2):
                if late:
                    own_tail(d, ends[d] == k)
                else:
                    tail(d, k)
            finish()
            if k == 1:
                y_wait(fld, sems, 0, 0)
                for d in range(2):
                    if asym:
                        @pl.when(corner[d])
                        def _():
                            side_copy(fld, sems, 1 - d, bulk).start()
                    if shift:
                        @pl.when(near[d])
                        def _():
                            side_copy(fld, sems, 1 - d, shift).start()
                todo.extend(bulk_work(fld, shard(z, 0, 0) + (1 - y), fetch))
                todo.extend(tail_work(fld, shard(z, 0, 0)))
            for d in range(2):
                when_has(d, k, bulk_work(fld, shard(z, d, k) + y, fetch))
                if k > 1 and not late:
                    others(d, k - 1, z_has(d, k - 1))
        finish()
        if late:
            for k in range(1, levels):
                for d in range(2):
                    if k < top:
                        others(d, k, corner[d])
                for d in range(2):
                    tail(d, k)
                if k == top - 1:
                    finish()
            finish()
            for k in range(1, top):
                for d in range(2):
                    others(d, k, z_has(d, k) & jnp.logical_not(corner[d]))
        for d in range(2):
            others(d, top, z_has(d, top))
        finish()

    def drain(fld, sems, asym, shift):
        def sent(sem, rsem, dev, count):
            view = fld[0].at[pl.ds(0, count)]
            remote(view, view, sem, rsem, dev).wait_send()

        full = rt + top * bulk
        ending = corner[0] | corner[1]

        @pl.when(ending)
        def _():
            sent(sems[2], sems[3].at[0], y_dev, full - shift)

        @pl.when(jnp.logical_not(ending))
        def _():
            sent(sems[2], sems[3].at[0], y_dev, full - bulk if asym else full)

        for d in range(2):
            for k in range(top):
                plain = z_has(d, k) & can[d]
                if k == 0:
                    for more, when in ((bulk if asym else 0, corner[1 - d]), (shift, near[1 - d])):
                        @pl.when(plain & when)
                        def _():
                            sent(z_sent(sems, d, k), sems[1].at[0, 0], z_dev[d], bulk + 2 + more)
                    plain = plain & jnp.logical_not(corner[1 - d] | near[1 - d])

                @pl.when(plain)
                def _():
                    sent(z_sent(sems, d, k), sems[1].at[0, 0], z_dev[d], bulk + 2)

    half = rt * tile // 2
    fld1, fld2 = (main1, last1), (main2, last2)
    sems1 = (zs1, zr1, ys1, yr1)
    sems2 = (zs2, zr2, ys2, yr2)
    bias = bias_v[:, pl.ds(pl.multiple_of(mc * tile, tile), tile)]
    for s in range(4):
        w_copy(s).wait()

    def mixed_rows(c):
        return jnp.concatenate([f_ref[c], fall[0, c], fall[1, c], fall[2, c]], axis=1)

    def mix(c):
        both = jnp.concatenate([w_v[o].reshape(4 * tile, tile) for o in range(2)], axis=1)
        r = jnp.dot(mixed_rows(c), both, preferred_element_type=F32)
        rows = pl.ds(c * tile, tile)
        base[rows, :] = base[rows, :] + r[:, :tile]
        fw1[rows, :] = r[:, tile:]

    blocks_left = list(range(2 * levels))
    for _ in range(2):
        fetch_block(blocks_left.pop(0))
    def pass_on(c):
        x_copy(1, c).wait_recv()
        x_copy(2, c).start()

    pass_on(order[0])
    for i, c in enumerate(order):
        if i + 1 < rt:
            pass_on(order[i + 1])
        x_copy(0, c).wait_recv()
        x_copy(2, c).wait_recv()
        r = jnp.dot(mixed_rows(c), w_v[2].reshape(4 * tile, tile), preferred_element_type=F32)
        at(fld1, me, c)[...] = r.astype(BF16)
        emit_own(fld1, sems1, c)
        rows = pl.ds(c * tile, tile)
        base[rows, :] = bias - r
        if blocks_left:
            fetch_block(blocks_left.pop(0))

    for t in range(rt):
        total = jnp.sum(sq[tab[2 + pair_rows, t]], axis=1, keepdims=True)
        inv[pl.ds(t * tile, tile), :] = jnp.broadcast_to(lax.rsqrt(1.0 + total), (tile, tile))

    for block in blocks_left:
        fetch_block(block)
    gather(fld1, sems1, [functools.partial(mix, c) for c in range(rt)], True, True, 0)
    for c in order:
        rows = pl.ds(c * tile, tile)
        at(fld2, me, c)[...] = (fw1[rows, :] + 2.0 * (acc[rows, :] * inv[rows, :])).astype(BF16)
        emit_own(fld2, sems2, c)
    gather(fld2, sems2, [], True, False, 0)
    out_ref[...] = (base[...] + acc[...] * inv[...]).astype(BF16)
    for kind in range(3):
        remote(f_ref, f_ref, xs.at[kind], xr.at[kind, 0], partner).wait_send()
    drain(fld1, sems1, True, 0)
    drain(fld2, sems2, False, 0)


def fast(features, tile_values, tile_source, tile_target, tile_count, weights, bias_vector):
    slots, tile, _ = tile_values.shape
    rows, cols = features.shape
    rt = rows // tile
    blocks = lax.axis_size("blk")
    levels = blocks // 2
    vmem = pl.BlockSpec(memory_space=pltpu.VMEM)
    hbm = pl.BlockSpec(memory_space=pltpu.HBM)
    dma = pltpu.SemaphoreType.DMA
    gather_sems = [
        dma((levels + 1,)), dma((levels, rt)), dma, dma((levels + 1,)),
    ]
    return pl.pallas_call(
        functools.partial(fast_kernel, levels),
        out_shape=jax.ShapeDtypeStruct((rows, cols), BF16),
        in_specs=[hbm] * 6,
        out_specs=vmem,
        scratch_shapes=[
            pltpu.VMEM((rt, tile, tile), BF16),
            pltpu.VMEM((3, rt, tile, tile), BF16),
            pltpu.VMEM((blocks * (rt - 1), tile, tile), BF16),
            pltpu.VMEM((blocks, tile, tile), BF16),
            pltpu.VMEM((blocks * (rt - 1), tile, tile), BF16),
            pltpu.VMEM((blocks, tile, tile), BF16),
            pltpu.VMEM((slots + 1, tile, tile), BF16),
            pltpu.VMEM((slots + 1, tile, tile), F32),
            pltpu.VMEM((blocks, rows, rows), BF16),
            pltpu.VMEM((3, 4, tile, tile), BF16),
            pltpu.VMEM((rows, tile), F32),
            pltpu.VMEM((rows, tile), F32),
            pltpu.VMEM((rows, tile), F32),
            pltpu.VMEM((rows, tile), F32),
            pltpu.VMEM((8, tile), jnp.int32),
            pltpu.VMEM((8, slots), jnp.int32),
            pltpu.SMEM((8, slots), jnp.int32),
            pltpu.VMEM((1, 4 * cols), F32),
            dma, dma, dma((3,)), dma, dma((4,)), dma((3,)), dma((3, rt)),
        ] + gather_sems + gather_sems,
        compiler_params=pltpu.CompilerParams(collective_id=0, has_side_effects=True, vmem_limit_bytes=58 << 20),
        name="propagate",
    )(
        features.reshape(rt, tile, cols), tile_values, tile_source.reshape(1, -1), tile_target.reshape(1, -1),
        weights, bias_vector.reshape(1, -1),
    )


def per_device(features, tile_values, tile_source, tile_target, tile_count, weights, bias_vector):
    tile_size = tile_values.shape[1]
    slot_total = tile_values.shape[0]
    channels = features.shape[1]
    row_tiles = features.shape[0] // tile_size
    block_rows = row_tiles * tile_size
    block_count = lax.axis_size("blk")
    slot_cap = max(2, (2 * slot_total + block_count - 1) // block_count)
    usable = jnp.arange(slot_total, dtype=jnp.int32) < tile_count[0]
    squares = jnp.einsum(
        "tij,tij->ti", tile_values, tile_values, preferred_element_type=jnp.float32
    )
    squares = jnp.where(usable[:, None], squares, 0.0)
    onehot = (
        (tile_target[:, None] == jnp.arange(row_tiles, dtype=jnp.int32)[None, :]) & usable[:, None]
    ).astype(jnp.float32)
    row_norm = jnp.dot(onehot.T, squares, precision=lax.Precision.HIGHEST)
    inverse = lax.rsqrt(1.0 + row_norm).reshape(-1)
    zero_sum = jnp.zeros((row_tiles, tile_size, channels), jnp.float32)

    def cycle_prop(signal):
        segment = lax.all_gather(signal, "blk", axis=0, tiled=True)
        offset = jnp.int32(0)
        count_rows = segment.shape[0]
        window = min(slot_total, slot_cap * (count_rows // block_rows + 2))
        low_row = tile_source * tile_size
        first_slot = jnp.sum(usable & (low_row + tile_size <= offset))
        end_slot = jnp.sum(usable & (low_row < offset + count_rows))
        start_slot = jnp.minimum(first_slot, slot_total - window)
        slot_ids = start_slot + jnp.arange(window, dtype=jnp.int32)
        in_range = (slot_ids >= first_slot) & (slot_ids < end_slot)
        row_ids = tile_source[:, None] * tile_size + jnp.arange(tile_size, dtype=jnp.int32)[None, :]
        inside = (row_ids >= 0) & (row_ids < count_rows) & in_range[:, None]
        picked = jnp.take(segment, jnp.clip(row_ids, 0, count_rows - 1).reshape(-1), axis=0)
        picked = picked.reshape(window, tile_size, channels)
        picked = jnp.where(inside[:, :, None], picked, jnp.zeros((), segment.dtype))
        product = jnp.einsum(
            "gij,gjc->gic", tile_values, picked, preferred_element_type=jnp.float32
        )
        product = jnp.where(in_range[:, None, None], product, 0.0)
        summed = zero_sum.at[tile_target].add(product)
        return summed.reshape(-1, channels) * inverse[:, None]

    col_start = lax.axis_index("ch") * channels
    bias_part = lax.dynamic_slice_in_dim(bias_vector, col_start, channels, 0)
    w_cols = lax.dynamic_slice_in_dim(weights, col_start, channels, 2)

    def mix_term(order_term, order_index, running):
        w_slice = w_cols[order_index]
        return running + jnp.dot(
            lax.all_gather(order_term, "ch", axis=1, tiled=True),
            w_slice,
            preferred_element_type=jnp.float32,
        )

    result = mix_term(features, 0, jnp.zeros((features.shape[0], channels), jnp.float32))
    first_order = cycle_prop(features).astype(jnp.bfloat16)
    result = mix_term(first_order, 1, result)
    second_order = (2.0 * cycle_prop(first_order) - features.astype(jnp.float32)).astype(
        jnp.bfloat16
    )
    result = mix_term(second_order, 2, result)
    return (result + bias_part[None, :]).astype(jnp.bfloat16)


def solution(mesh):
    dense = mesh.shape["blk"] == 8 and mesh.shape["ch"] == 4
    return jax.shard_map(
        fast if dense else per_device,
        mesh=mesh,
        in_specs=(P("blk", "ch"), P("blk", None, None), P("blk"), P("blk"), P("blk"), P(), P()),
        out_specs=P("blk", "ch"),
        check_vma=False,
    )
```

```python
import functools

import jax
import jax.numpy as jnp
from jax import lax
from jax.experimental import pallas as pl
from jax.experimental.pallas import tpu as pltpu
from jax.sharding import PartitionSpec as P

MESH = pl.DeviceIdType.MESH
F32 = jnp.float32
BF16 = jnp.bfloat16
def fast_kernel(
    levels, f_any, tiles_any, src_any, tgt_any, w_any, bias_any, out_ref,
    f_ref, fall, main1, last1, main2, last2, tiles, sq, a_v, w_v, acc, base, fw1, inv, ints, tab_v, tab, bias_v,
    fsem, tsem, isem, psem, wsem, xs, xr, zs1, zr1, ys1, yr1, zs2, zr2, ys2, yr2,
):
    rt, tile = f_ref.shape[0], f_ref.shape[1]
    bulk = rt - 1
    slots = tiles_any.shape[0]
    top = levels - 1
    me, mc = lax.axis_index("blk"), lax.axis_index("ch")
    z, y = lax.div(me, 2), lax.rem(me, 2)
    x, core = lax.div(mc, 2), lax.rem(mc, 2)
    partner = (me, 2 * x + (1 - core))
    across = (me, 2 * (1 - x) + core)
    y_dev = (2 * z + (1 - y), mc)
    z_dev = ((me + 2, mc), (me - 2, mc))
    can = (z < top, z > 0)

    barrier = pltpu.get_barrier_semaphore()
    for dev in (partner, across, y_dev):
        pl.semaphore_signal(barrier, inc=1, device_id=dev, device_id_type=MESH)
    for d in range(2):
        @pl.when(can[d])
        def _():
            pl.semaphore_signal(barrier, inc=1, device_id=z_dev[d], device_id_type=MESH)

    f_copy = pltpu.make_async_copy(f_any, f_ref, fsem)
    f_copy.start()
    int_copies = [
        pltpu.make_async_copy(src_any, ints.at[pl.ds(0, 1)], isem.at[0]),
        pltpu.make_async_copy(tgt_any, ints.at[pl.ds(1, 1)], isem.at[1]),
        pltpu.make_async_copy(bias_any, bias_v, isem.at[2]),
    ]
    for copy in int_copies:
        copy.start()
    tile_copy = pltpu.make_async_copy(tiles_any, tiles.at[pl.ds(0, slots)], tsem)
    tile_copy.start()
    order_of = (mc, partner[1], across[1], 2 * (1 - x) + (1 - core))

    def w_copy(s):
        q = pl.multiple_of(order_of[s] * tile, tile)
        p = pl.multiple_of(mc * tile, tile)
        return pltpu.make_async_copy(w_any.at[:, pl.ds(q, tile), pl.ds(p, tile)], w_v.at[:, s], wsem.at[s])

    for s in range(4):
        w_copy(s).start()

    tiles[slots] = jnp.zeros((tile, tile), BF16)
    sq[slots] = jnp.zeros((tile, tile), F32)

    for copy in int_copies:
        copy.wait()
    lane = lax.broadcasted_iota(jnp.int32, (slots, slots), 1)
    sub = lax.broadcasted_iota(jnp.int32, (slots, slots), 0)
    src_r, tgt_r = ints[0:1, :], ints[1:2, :]
    live = src_r < 2 * levels * rt
    key = jnp.broadcast_to(jnp.where(live, src_r * 8 + tgt_r, -1), (slots, slots))
    key_t = key.T
    target = jnp.broadcast_to(jnp.where(live, tgt_r, -1), (slots, slots))
    target_t = target.T

    def latest(hit):
        found = jnp.max(jnp.where(hit, sub, -1), axis=0, keepdims=True)
        return jnp.where(found < 0, slots, found)

    tab_v[0:1, :] = latest((key_t == key) & (sub < lane))
    tab_v[1:2, :] = latest((target_t == target) & (sub < lane))
    pair_rows = (2 * levels * rt * 8) // slots
    for i in range(pair_rows):
        tab_v[2 + i : 3 + i, :] = latest(key_t == lane + i * slots)
    tab_v[2 + pair_rows : 3 + pair_rows, :] = latest(target_t == lane)
    tab_copy = pltpu.make_async_copy(tab_v, tab, psem)
    tab_copy.start()
    f_copy.wait()

    pl.semaphore_wait(barrier, 3 + can[0].astype(jnp.int32) + can[1].astype(jnp.int32))

    def remote(src, dst, ssem, rsem, dev):
        return pltpu.make_async_remote_copy(
            src_ref=src, dst_ref=dst, send_sem=ssem, recv_sem=rsem, device_id=dev, device_id_type=MESH
        )

    def x_copy(kind, c):
        src = f_ref.at[c] if kind < 2 else fall.at[1, c]
        return remote(
            src, fall.at[kind, c], xs.at[kind], xr.at[kind, c], across if kind == 1 else partner
        )

    order = [0, rt - 1] + list(range(1, rt - 1))
    for c in order:
        x_copy(1, c).start()
        x_copy(0, c).start()

    tab_copy.wait()
    tile_copy.wait()

    def chain(k, _):
        value = tiles[k]
        wide = value.astype(F32)
        sq[k] = sq[tab[1, k]] + wide * wide
        tiles[k] = (wide + tiles[tab[0, k]].astype(F32)).astype(BF16)
        return 0

    lax.fori_loop(0, slots, chain, 0, unroll=2)

    def at(fld, block, it):
        return fld[0].at[block * bulk + it] if it < bulk else fld[1].at[block]

    def level_of(d, k):
        return z - k if d == 0 else z + k

    def shard(z0, d, k):
        return 2 * level_of(d, k)

    def z_view(fld, d, k, it):
        pair = shard(z, d, k)
        return at(fld, pair + y, it) if it < bulk else fld[1].at[pl.ds(pair, 2)]

    def z_copy(fld, sems, d, k, it):
        view = z_view(fld, d, k, it)
        level = level_of(d, k)
        return remote(view, view, z_sent(sems, d, k), sems[1].at[level, it], z_dev[d])

    def side_copy(fld, sems, d, count):
        view = fld[0].at[pl.ds((shard(z, 0, 0) + (1 - y)) * bulk, count)]
        return remote(view, view, z_sent(sems, d, 0), sems[3].at[z], z_dev[d])

    def z_wait(fld, sems, d, k, it):
        view = z_view(fld, d, k, it)
        remote(view, view, sems[0].at[0], sems[1].at[level_of(d, k), it], y_dev).wait_recv()

    def z_has(d, k):
        return z - k >= 0 if d == 0 else z + k <= top

    def z_sent(sems, d, k):
        return sems[0].at[level_of(d, k) if k or d else levels]

    def y_copy(fld, sems, d, k, it):
        view = at(fld, shard(z, d, k) + y, it)
        sem = level_of(d, k) if it < bulk else levels
        return remote(view, view, sems[2], sems[3].at[sem], y_dev)

    def y_wait(fld, sems, d, k, last=False):
        other = shard(z, d, k) + (1 - y)
        view = fld[1].at[other] if last else fld[0].at[pl.ds(other * bulk, bulk)]
        sem = levels if last else level_of(d, k)
        remote(view, view, sems[2], sems[3].at[sem], y_dev).wait_recv()

    def fetch_block(block):
        for t in range(rt):
            for s in range(rt):
                spot = (block * rt + s) * 8 + t
                slot = tab[2 + lax.div(spot, slots), lax.rem(spot, slots)]
                a_v[block, t * tile : (t + 1) * tile, s * tile : (s + 1) * tile] = tiles[slot]

    def add(h, lhs, rhs, init):
        product = jnp.dot(lhs, rhs, preferred_element_type=F32)
        rows = slice(h * half, (h + 1) * half)
        acc[rows, :] = product if init else acc[rows, :] + product

    def bulk_half(fld, block, h, init=False):
        rhs = fld[0][pl.ds(block * bulk, bulk)].reshape(bulk * tile, tile)
        add(h, a_v[block, h * half : (h + 1) * half, : bulk * tile], rhs, init)

    def tail_half(fld, pair, h):
        lhs = [a_v[pair + i, h * half : (h + 1) * half, bulk * tile :] for i in range(2)]
        rhs = fld[1][pl.ds(pair, 2)].reshape(2 * tile, tile)
        add(h, jnp.concatenate(lhs, axis=1), rhs, False)

    def bulk_work(fld, block, fetch, init=False):
        first = [lambda: fetch_block(block)] if fetch else []
        return first + [lambda h=h: bulk_half(fld, block, h, init) for h in range(1)]

    def tail_work(fld, pair):
        return [lambda h=h: tail_half(fld, pair, h) for h in range(1)]

    def emit_own(fld, sems, c):
        y_copy(fld, sems, 0, 0, c).start()
        if c < bulk:
            for d in range(2):
                @pl.when(can[d])
                def _():
                    z_copy(fld, sems, d, 0, c).start()

    corner = (z == top, z == 0)
    near = (z == 1, z == top - 1)

    def gather(fld, sems, extra, late, asym, shift):
        fetch = False
        todo = bulk_work(fld, me, fetch, True) + extra

        def step():
            if todo:
                todo.pop(0)()

        def when_has(d, k, work):
            def go(w):
                @pl.when(z_has(d, k))
                def _():
                    w()
            todo.extend([functools.partial(go, w) for w in work])

        def finish():
            while todo:
                step()

        def own_tail(d, ready):
            @pl.when(can[d] & ready)
            def _():
                z_copy(fld, sems, d, 0, bulk).start()

        def tail(d, k):
            @pl.when(z_has(d, k))
            def _():
                z_wait(fld, sems, d, k, bulk)
                if k < top:
                    @pl.when(can[d])
                    def _():
                        z_copy(fld, sems, d, k, bulk).start()
            when_has(d, k, tail_work(fld, shard(z, d, k)))

        def others(d, k, when):
            @pl.when(when)
            def _():
                y_wait(fld, sems, d, k)
                for w in bulk_work(fld, shard(z, d, k) + (1 - y), fetch):
                    w()

        ends = (z, top - z)
        for k in range(1, levels):
            for it in range(bulk):
                step()
                for d in range(2):
                    @pl.when(z_has(d, k))
                    def _():
                        z_wait(fld, sems, d, k, it)
                        if k == 1:
                            skip = near[d] if asym else z < 0
                            if it < shift:
                                skip = skip | corner[d]

                            @pl.when(jnp.logical_not(skip))
                            def _():
                                y_copy(fld, sems, d, k, it).start()
                        else:
                            y_copy(fld, sems, d, k, it).start()
                        if k < top:
                            @pl.when(can[d])
                            def _():
                                z_copy(fld, sems, d, k, it).start()
                if k == 1 and it == 1:
                    y_wait(fld, sems, 0, 0, True)
                    for d in range(2):
                        own_tail(d, ends[d] == 0 if late else True)
            for d in range(2):
                if late:
                    own_tail(d, ends[d] == k)
                else:
                    tail(d, k)
            finish()
            if k == 1:
                y_wait(fld, sems, 0, 0)
                for d in range(2):
                    if asym:
                        @pl.when(corner[d])
                        def _():
                            side_copy(fld, sems, 1 - d, bulk).start()
                    if shift:
                        @pl.when(near[d])
                        def _():
                            side_copy(fld, sems, 1 - d, shift).start()
                todo.extend(bulk_work(fld, shard(z, 0, 0) + (1 - y), fetch))
                todo.extend(tail_work(fld, shard(z, 0, 0)))
            for d in range(2):
                when_has(d, k, bulk_work(fld, shard(z, d, k) + y, fetch))
                if k > 1 and not late:
                    others(d, k - 1, z_has(d, k - 1))
        finish()
        if late:
            for k in range(1, levels):
                for d in range(2):
                    if k < top:
                        others(d, k, corner[d])
                for d in range(2):
                    tail(d, k)
                if k == top - 1:
                    finish()
            finish()
            for k in range(1, top):
                for d in range(2):
                    others(d, k, z_has(d, k) & jnp.logical_not(corner[d]))
        for d in range(2):
            others(d, top, z_has(d, top))
        finish()

    def drain(fld, sems, asym, shift):
        def sent(sem, rsem, dev, count):
            view = fld[0].at[pl.ds(0, count)]
            remote(view, view, sem, rsem, dev).wait_send()

        full = rt + top * bulk
        ending = corner[0] | corner[1]

        @pl.when(ending)
        def _():
            sent(sems[2], sems[3].at[0], y_dev, full - shift)

        @pl.when(jnp.logical_not(ending))
        def _():
            sent(sems[2], sems[3].at[0], y_dev, full - bulk if asym else full)

        for d in range(2):
            for k in range(top):
                plain = z_has(d, k) & can[d]
                if k == 0:
                    for more, when in ((bulk if asym else 0, corner[1 - d]), (shift, near[1 - d])):
                        @pl.when(plain & when)
                        def _():
                            sent(z_sent(sems, d, k), sems[1].at[0, 0], z_dev[d], bulk + 2 + more)
                    plain = plain & jnp.logical_not(corner[1 - d] | near[1 - d])

                @pl.when(plain)
                def _():
                    sent(z_sent(sems, d, k), sems[1].at[0, 0], z_dev[d], bulk + 2)

    half = rt * tile // 1
    fld1, fld2 = (main1, last1), (main2, last2)
    sems1 = (zs1, zr1, ys1, yr1)
    sems2 = (zs2, zr2, ys2, yr2)
    bias = bias_v[:, pl.ds(pl.multiple_of(mc * tile, tile), tile)]
    for s in range(4):
        w_copy(s).wait()

    def mixed_rows(c):
        return jnp.concatenate([f_ref[c], fall[0, c], fall[1, c], fall[2, c]], axis=1)

    def mix(c):
        both = jnp.concatenate([w_v[o].reshape(4 * tile, tile) for o in range(2)], axis=1)
        r = jnp.dot(mixed_rows(c), both, preferred_element_type=F32)
        rows = pl.ds(c * tile, tile)
        base[rows, :] = base[rows, :] + r[:, :tile]
        fw1[rows, :] = r[:, tile:]

    blocks_left = list(range(2 * levels))
    for _ in range(2):
        fetch_block(blocks_left.pop(0))
    def pass_on(c):
        x_copy(1, c).wait_recv()
        x_copy(2, c).start()

    pass_on(order[0])
    for i, c in enumerate(order):
        if i + 1 < rt:
            pass_on(order[i + 1])
        x_copy(0, c).wait_recv()
        x_copy(2, c).wait_recv()
        r = jnp.dot(mixed_rows(c), w_v[2].reshape(4 * tile, tile), preferred_element_type=F32)
        at(fld1, me, c)[...] = r.astype(BF16)
        emit_own(fld1, sems1, c)
        rows = pl.ds(c * tile, tile)
        base[rows, :] = bias - r
        if blocks_left:
            fetch_block(blocks_left.pop(0))

    for t in range(rt):
        total = jnp.sum(sq[tab[2 + pair_rows, t]], axis=1, keepdims=True)
        inv[pl.ds(t * tile, tile), :] = jnp.broadcast_to(lax.rsqrt(1.0 + total), (tile, tile))

    for block in blocks_left:
        fetch_block(block)
    gather(fld1, sems1, [functools.partial(mix, c) for c in range(rt)], True, True, 0)
    for c in order:
        rows = pl.ds(c * tile, tile)
        at(fld2, me, c)[...] = (fw1[rows, :] + 2.0 * (acc[rows, :] * inv[rows, :])).astype(BF16)
        emit_own(fld2, sems2, c)
    gather(fld2, sems2, [], True, False, 0)
    out_ref[...] = (base[...] + acc[...] * inv[...]).astype(BF16)
    for kind in range(3):
        remote(f_ref, f_ref, xs.at[kind], xr.at[kind, 0], partner).wait_send()
    drain(fld1, sems1, True, 0)
    drain(fld2, sems2, False, 0)


def fast(features, tile_values, tile_source, tile_target, tile_count, weights, bias_vector):
    slots, tile, _ = tile_values.shape
    rows, cols = features.shape
    rt = rows // tile
    blocks = lax.axis_size("blk")
    levels = blocks // 2
    vmem = pl.BlockSpec(memory_space=pltpu.VMEM)
    hbm = pl.BlockSpec(memory_space=pltpu.HBM)
    dma = pltpu.SemaphoreType.DMA
    gather_sems = [
        dma((levels + 1,)), dma((levels, rt)), dma, dma((levels + 1,)),
    ]
    return pl.pallas_call(
        functools.partial(fast_kernel, levels),
        out_shape=jax.ShapeDtypeStruct((rows, cols), BF16),
        in_specs=[hbm] * 6,
        out_specs=vmem,
        scratch_shapes=[
            pltpu.VMEM((rt, tile, tile), BF16),
            pltpu.VMEM((3, rt, tile, tile), BF16),
            pltpu.VMEM((blocks * (rt - 1), tile, tile), BF16),
            pltpu.VMEM((blocks, tile, tile), BF16),
            pltpu.VMEM((blocks * (rt - 1), tile, tile), BF16),
            pltpu.VMEM((blocks, tile, tile), BF16),
            pltpu.VMEM((slots + 1, tile, tile), BF16),
            pltpu.VMEM((slots + 1, tile, tile), F32),
            pltpu.VMEM((blocks, rows, rows), BF16),
            pltpu.VMEM((3, 4, tile, tile), BF16),
            pltpu.VMEM((rows, tile), F32),
            pltpu.VMEM((rows, tile), F32),
            pltpu.VMEM((rows, tile), F32),
            pltpu.VMEM((rows, tile), F32),
            pltpu.VMEM((8, tile), jnp.int32),
            pltpu.VMEM((8, slots), jnp.int32),
            pltpu.SMEM((8, slots), jnp.int32),
            pltpu.VMEM((1, 4 * cols), F32),
            dma, dma, dma((3,)), dma, dma((4,)), dma((3,)), dma((3, rt)),
        ] + gather_sems + gather_sems,
        compiler_params=pltpu.CompilerParams(collective_id=0, has_side_effects=True, vmem_limit_bytes=58 << 20),
        name="propagate",
    )(
        features.reshape(rt, tile, cols), tile_values, tile_source.reshape(1, -1), tile_target.reshape(1, -1),
        weights, bias_vector.reshape(1, -1),
    )


def per_device(features, tile_values, tile_source, tile_target, tile_count, weights, bias_vector):
    tile_size = tile_values.shape[1]
    slot_total = tile_values.shape[0]
    channels = features.shape[1]
    row_tiles = features.shape[0] // tile_size
    block_rows = row_tiles * tile_size
    block_count = lax.axis_size("blk")
    slot_cap = max(2, (2 * slot_total + block_count - 1) // block_count)
    usable = jnp.arange(slot_total, dtype=jnp.int32) < tile_count[0]
    squares = jnp.einsum(
        "tij,tij->ti", tile_values, tile_values, preferred_element_type=jnp.float32
    )
    squares = jnp.where(usable[:, None], squares, 0.0)
    onehot = (
        (tile_target[:, None] == jnp.arange(row_tiles, dtype=jnp.int32)[None, :]) & usable[:, None]
    ).astype(jnp.float32)
    row_norm = jnp.dot(onehot.T, squares, precision=lax.Precision.HIGHEST)
    inverse = lax.rsqrt(1.0 + row_norm).reshape(-1)
    zero_sum = jnp.zeros((row_tiles, tile_size, channels), jnp.float32)

    def cycle_prop(signal):
        segment = lax.all_gather(signal, "blk", axis=0, tiled=True)
        offset = jnp.int32(0)
        count_rows = segment.shape[0]
        window = min(slot_total, slot_cap * (count_rows // block_rows + 2))
        low_row = tile_source * tile_size
        first_slot = jnp.sum(usable & (low_row + tile_size <= offset))
        end_slot = jnp.sum(usable & (low_row < offset + count_rows))
        start_slot = jnp.minimum(first_slot, slot_total - window)
        slot_ids = start_slot + jnp.arange(window, dtype=jnp.int32)
        in_range = (slot_ids >= first_slot) & (slot_ids < end_slot)
        row_ids = tile_source[:, None] * tile_size + jnp.arange(tile_size, dtype=jnp.int32)[None, :]
        inside = (row_ids >= 0) & (row_ids < count_rows) & in_range[:, None]
        picked = jnp.take(segment, jnp.clip(row_ids, 0, count_rows - 1).reshape(-1), axis=0)
        picked = picked.reshape(window, tile_size, channels)
        picked = jnp.where(inside[:, :, None], picked, jnp.zeros((), segment.dtype))
        product = jnp.einsum(
            "gij,gjc->gic", tile_values, picked, preferred_element_type=jnp.float32
        )
        product = jnp.where(in_range[:, None, None], product, 0.0)
        summed = zero_sum.at[tile_target].add(product)
        return summed.reshape(-1, channels) * inverse[:, None]

    col_start = lax.axis_index("ch") * channels
    bias_part = lax.dynamic_slice_in_dim(bias_vector, col_start, channels, 0)
    w_cols = lax.dynamic_slice_in_dim(weights, col_start, channels, 2)

    def mix_term(order_term, order_index, running):
        w_slice = w_cols[order_index]
        return running + jnp.dot(
            lax.all_gather(order_term, "ch", axis=1, tiled=True),
            w_slice,
            preferred_element_type=jnp.float32,
        )

    result = mix_term(features, 0, jnp.zeros((features.shape[0], channels), jnp.float32))
    first_order = cycle_prop(features).astype(jnp.bfloat16)
    result = mix_term(first_order, 1, result)
    second_order = (2.0 * cycle_prop(first_order) - features.astype(jnp.float32)).astype(
        jnp.bfloat16
    )
    result = mix_term(second_order, 2, result)
    return (result + bias_part[None, :]).astype(jnp.bfloat16)


def solution(mesh):
    dense = mesh.shape["blk"] == 8 and mesh.shape["ch"] == 4
    return jax.shard_map(
        fast if dense else per_device,
        mesh=mesh,
        in_specs=(P("blk", "ch"), P("blk", None, None), P("blk"), P("blk"), P("blk"), P(), P()),
        out_specs=P("blk", "ch"),
        check_vma=False,
    )
```

```python
import functools

import jax
import jax.numpy as jnp
from jax import lax
from jax.experimental import pallas as pl
from jax.experimental.pallas import tpu as pltpu
from jax.sharding import PartitionSpec as P

MESH = pl.DeviceIdType.MESH
F32 = jnp.float32
BF16 = jnp.bfloat16
def fast_kernel(
    levels, f_any, tiles_any, src_any, tgt_any, w_any, bias_any, out_ref,
    f_ref, fall, main1, last1, main2, last2, tiles, sq, a_v, w_v, acc, base, fw1, inv, ints, tab_v, tab, bias_v,
    fsem, tsem, isem, psem, wsem, xs, xr, zs1, zr1, ys1, yr1, zs2, zr2, ys2, yr2,
):
    rt, tile = f_ref.shape[0], f_ref.shape[1]
    bulk = rt - 1
    slots = tiles_any.shape[0]
    top = levels - 1
    me, mc = lax.axis_index("blk"), lax.axis_index("ch")
    z, y = lax.div(me, 2), lax.rem(me, 2)
    x, core = lax.div(mc, 2), lax.rem(mc, 2)
    partner = (me, 2 * x + (1 - core))
    across = (me, 2 * (1 - x) + core)
    y_dev = (2 * z + (1 - y), mc)
    z_dev = ((me + 2, mc), (me - 2, mc))
    can = (z < top, z > 0)

    barrier = pltpu.get_barrier_semaphore()
    for dev in (partner, across, y_dev):
        pl.semaphore_signal(barrier, inc=1, device_id=dev, device_id_type=MESH)
    for d in range(2):
        @pl.when(can[d])
        def _():
            pl.semaphore_signal(barrier, inc=1, device_id=z_dev[d], device_id_type=MESH)

    f_copy = pltpu.make_async_copy(f_any, f_ref, fsem)
    f_copy.start()
    int_copies = [
        pltpu.make_async_copy(src_any, ints.at[pl.ds(0, 1)], isem.at[0]),
        pltpu.make_async_copy(tgt_any, ints.at[pl.ds(1, 1)], isem.at[1]),
        pltpu.make_async_copy(bias_any, bias_v, isem.at[2]),
    ]
    for copy in int_copies:
        copy.start()
    tile_copy = pltpu.make_async_copy(tiles_any, tiles.at[pl.ds(0, slots)], tsem)
    tile_copy.start()
    order_of = (mc, partner[1], across[1], 2 * (1 - x) + (1 - core))

    def w_copy(s):
        q = pl.multiple_of(order_of[s] * tile, tile)
        p = pl.multiple_of(mc * tile, tile)
        return pltpu.make_async_copy(w_any.at[:, pl.ds(q, tile), pl.ds(p, tile)], w_v.at[:, s], wsem.at[s])

    for s in range(4):
        w_copy(s).start()

    tiles[slots] = jnp.zeros((tile, tile), BF16)
    sq[slots] = jnp.zeros((tile, tile), F32)

    for copy in int_copies:
        copy.wait()
    lane = lax.broadcasted_iota(jnp.int32, (slots, slots), 1)
    sub = lax.broadcasted_iota(jnp.int32, (slots, slots), 0)
    src_r, tgt_r = ints[0:1, :], ints[1:2, :]
    live = src_r < 2 * levels * rt
    key = jnp.broadcast_to(jnp.where(live, src_r * 8 + tgt_r, -1), (slots, slots))
    key_t = key.T
    target = jnp.broadcast_to(jnp.where(live, tgt_r, -1), (slots, slots))
    target_t = target.T

    def latest(hit):
        found = jnp.max(jnp.where(hit, sub, -1), axis=0, keepdims=True)
        return jnp.where(found < 0, slots, found)

    tab_v[0:1, :] = latest((key_t == key) & (sub < lane))
    tab_v[1:2, :] = latest((target_t == target) & (sub < lane))
    pair_rows = (2 * levels * rt * 8) // slots
    for i in range(pair_rows):
        tab_v[2 + i : 3 + i, :] = latest(key_t == lane + i * slots)
    tab_v[2 + pair_rows : 3 + pair_rows, :] = latest(target_t == lane)
    tab_copy = pltpu.make_async_copy(tab_v, tab, psem)
    tab_copy.start()
    f_copy.wait()

    pl.semaphore_wait(barrier, 3 + can[0].astype(jnp.int32) + can[1].astype(jnp.int32))

    def remote(src, dst, ssem, rsem, dev):
        return pltpu.make_async_remote_copy(
            src_ref=src, dst_ref=dst, send_sem=ssem, recv_sem=rsem, device_id=dev, device_id_type=MESH
        )

    def x_copy(kind, c):
        src = f_ref.at[c] if kind < 2 else fall.at[1, c]
        return remote(
            src, fall.at[kind, c], xs.at[kind], xr.at[kind, c], across if kind == 1 else partner
        )

    order = [0, 1, rt - 1] + list(range(2, rt - 1))
    for c in order:
        x_copy(1, c).start()
        x_copy(0, c).start()

    tab_copy.wait()
    tile_copy.wait()

    def chain(k, _):
        value = tiles[k]
        wide = value.astype(F32)
        sq[k] = sq[tab[1, k]] + wide * wide
        tiles[k] = (wide + tiles[tab[0, k]].astype(F32)).astype(BF16)
        return 0

    lax.fori_loop(0, slots, chain, 0, unroll=2)

    def at(fld, block, it):
        return fld[0].at[block * bulk + it] if it < bulk else fld[1].at[block]

    def level_of(d, k):
        return z - k if d == 0 else z + k

    def shard(z0, d, k):
        return 2 * level_of(d, k)

    def z_view(fld, d, k, it):
        pair = shard(z, d, k)
        return at(fld, pair + y, it) if it < bulk else fld[1].at[pl.ds(pair, 2)]

    def z_copy(fld, sems, d, k, it):
        view = z_view(fld, d, k, it)
        level = level_of(d, k)
        return remote(view, view, z_sent(sems, d, k), sems[1].at[level, it], z_dev[d])

    def side_copy(fld, sems, d, count):
        view = fld[0].at[pl.ds((shard(z, 0, 0) + (1 - y)) * bulk, count)]
        return remote(view, view, z_sent(sems, d, 0), sems[3].at[z], z_dev[d])

    def z_wait(fld, sems, d, k, it):
        view = z_view(fld, d, k, it)
        remote(view, view, sems[0].at[0], sems[1].at[level_of(d, k), it], y_dev).wait_recv()

    def z_has(d, k):
        return z - k >= 0 if d == 0 else z + k <= top

    def z_sent(sems, d, k):
        return sems[0].at[level_of(d, k) if k or d else levels]

    def y_copy(fld, sems, d, k, it):
        view = at(fld, shard(z, d, k) + y, it)
        sem = level_of(d, k) if it < bulk else levels
        return remote(view, view, sems[2], sems[3].at[sem], y_dev)

    def y_wait(fld, sems, d, k, last=False):
        other = shard(z, d, k) + (1 - y)
        view = fld[1].at[other] if last else fld[0].at[pl.ds(other * bulk, bulk)]
        sem = levels if last else level_of(d, k)
        remote(view, view, sems[2], sems[3].at[sem], y_dev).wait_recv()

    def fetch_block(block):
        for t in range(rt):
            for s in range(rt):
                spot = (block * rt + s) * 8 + t
                slot = tab[2 + lax.div(spot, slots), lax.rem(spot, slots)]
                a_v[block, t * tile : (t + 1) * tile, s * tile : (s + 1) * tile] = tiles[slot]

    def add(h, lhs, rhs, init):
        product = jnp.dot(lhs, rhs, preferred_element_type=F32)
        rows = slice(h * half, (h + 1) * half)
        acc[rows, :] = product if init else acc[rows, :] + product

    def bulk_half(fld, block, h, init=False):
        rhs = fld[0][pl.ds(block * bulk, bulk)].reshape(bulk * tile, tile)
        add(h, a_v[block, h * half : (h + 1) * half, : bulk * tile], rhs, init)

    def tail_half(fld, pair, h):
        lhs = [a_v[pair + i, h * half : (h + 1) * half, bulk * tile :] for i in range(2)]
        rhs = fld[1][pl.ds(pair, 2)].reshape(2 * tile, tile)
        add(h, jnp.concatenate(lhs, axis=1), rhs, False)

    def bulk_work(fld, block, fetch, init=False):
        first = [lambda: fetch_block(block)] if fetch else []
        return first + [lambda h=h: bulk_half(fld, block, h, init) for h in range(1)]

    def tail_work(fld, pair):
        return [lambda h=h: tail_half(fld, pair, h) for h in range(1)]

    def emit_own(fld, sems, c):
        y_copy(fld, sems, 0, 0, c).start()
        if c < bulk:
            for d in range(2):
                @pl.when(can[d])
                def _():
                    z_copy(fld, sems, d, 0, c).start()

    corner = (z == top, z == 0)
    near = (z == 1, z == top - 1)

    def gather(fld, sems, extra, late, asym, shift):
        fetch = False
        todo = bulk_work(fld, me, fetch, True) + extra

        def step():
            if todo:
                todo.pop(0)()

        def when_has(d, k, work):
            def go(w):
                @pl.when(z_has(d, k))
                def _():
                    w()
            todo.extend([functools.partial(go, w) for w in work])

        def finish():
            while todo:
                step()

        def own_tail(d, ready):
            @pl.when(can[d] & ready)
            def _():
                z_copy(fld, sems, d, 0, bulk).start()

        def tail(d, k):
            @pl.when(z_has(d, k))
            def _():
                z_wait(fld, sems, d, k, bulk)
                if k < top:
                    @pl.when(can[d])
                    def _():
                        z_copy(fld, sems, d, k, bulk).start()
            when_has(d, k, tail_work(fld, shard(z, d, k)))

        def others(d, k, when):
            @pl.when(when)
            def _():
                y_wait(fld, sems, d, k)
                for w in bulk_work(fld, shard(z, d, k) + (1 - y), fetch):
                    w()

        ends = (z, top - z)
        for k in range(1, levels):
            for it in range(bulk):
                step()
                for d in range(2):
                    @pl.when(z_has(d, k))
                    def _():
                        z_wait(fld, sems, d, k, it)
                        if k == 1:
                            skip = near[d] if asym else z < 0
                            if it < shift:
                                skip = skip | corner[d]

                            @pl.when(jnp.logical_not(skip))
                            def _():
                                y_copy(fld, sems, d, k, it).start()
                        else:
                            y_copy(fld, sems, d, k, it).start()
                        if k < top:
                            @pl.when(can[d])
                            def _():
                                z_copy(fld, sems, d, k, it).start()
                if k == 1 and it == 2:
                    y_wait(fld, sems, 0, 0, True)
                    for d in range(2):
                        own_tail(d, ends[d] == 0 if late else True)
            for d in range(2):
                if late:
                    own_tail(d, ends[d] == k)
                else:
                    tail(d, k)
            finish()
            if k == 1:
                y_wait(fld, sems, 0, 0)
                for d in range(2):
                    if asym:
                        @pl.when(corner[d])
                        def _():
                            side_copy(fld, sems, 1 - d, bulk).start()
                    if shift:
                        @pl.when(near[d])
                        def _():
                            side_copy(fld, sems, 1 - d, shift).start()
                todo.extend(bulk_work(fld, shard(z, 0, 0) + (1 - y), fetch))
                todo.extend(tail_work(fld, shard(z, 0, 0)))
            for d in range(2):
                when_has(d, k, bulk_work(fld, shard(z, d, k) + y, fetch))
                if k > 1 and not late:
                    others(d, k - 1, z_has(d, k - 1))
        finish()
        if late:
            for k in range(1, levels):
                for d in range(2):
                    if k < top:
                        others(d, k, corner[d])
                for d in range(2):
                    tail(d, k)
                if k == top - 1:
                    finish()
            finish()
            for k in range(1, top):
                for d in range(2):
                    others(d, k, z_has(d, k) & jnp.logical_not(corner[d]))
        for d in range(2):
            others(d, top, z_has(d, top))
        finish()

    def drain(fld, sems, asym, shift):
        def sent(sem, rsem, dev, count):
            view = fld[0].at[pl.ds(0, count)]
            remote(view, view, sem, rsem, dev).wait_send()

        full = rt + top * bulk
        ending = corner[0] | corner[1]

        @pl.when(ending)
        def _():
            sent(sems[2], sems[3].at[0], y_dev, full - shift)

        @pl.when(jnp.logical_not(ending))
        def _():
            sent(sems[2], sems[3].at[0], y_dev, full - bulk if asym else full)

        for d in range(2):
            for k in range(top):
                plain = z_has(d, k) & can[d]
                if k == 0:
                    for more, when in ((bulk if asym else 0, corner[1 - d]), (shift, near[1 - d])):
                        @pl.when(plain & when)
                        def _():
                            sent(z_sent(sems, d, k), sems[1].at[0, 0], z_dev[d], bulk + 2 + more)
                    plain = plain & jnp.logical_not(corner[1 - d] | near[1 - d])

                @pl.when(plain)
                def _():
                    sent(z_sent(sems, d, k), sems[1].at[0, 0], z_dev[d], bulk + 2)

    half = rt * tile // 1
    fld1, fld2 = (main1, last1), (main2, last2)
    sems1 = (zs1, zr1, ys1, yr1)
    sems2 = (zs2, zr2, ys2, yr2)
    bias = bias_v[:, pl.ds(pl.multiple_of(mc * tile, tile), tile)]
    for s in range(4):
        w_copy(s).wait()

    def mixed_rows(c):
        return jnp.concatenate([f_ref[c], fall[0, c], fall[1, c], fall[2, c]], axis=1)

    def mix(c):
        both = jnp.concatenate([w_v[o].reshape(4 * tile, tile) for o in range(2)], axis=1)
        r = jnp.dot(mixed_rows(c), both, preferred_element_type=F32)
        rows = pl.ds(c * tile, tile)
        base[rows, :] = base[rows, :] + r[:, :tile]
        fw1[rows, :] = r[:, tile:]

    blocks_left = list(range(2 * levels))
    for _ in range(2):
        fetch_block(blocks_left.pop(0))
    def pass_on(c):
        x_copy(1, c).wait_recv()
        x_copy(2, c).start()

    pass_on(order[0])
    for i, c in enumerate(order):
        if i + 1 < rt:
            pass_on(order[i + 1])
        x_copy(0, c).wait_recv()
        x_copy(2, c).wait_recv()
        r = jnp.dot(mixed_rows(c), w_v[2].reshape(4 * tile, tile), preferred_element_type=F32)
        at(fld1, me, c)[...] = r.astype(BF16)
        emit_own(fld1, sems1, c)
        rows = pl.ds(c * tile, tile)
        base[rows, :] = bias - r
        if blocks_left:
            fetch_block(blocks_left.pop(0))

    for t in range(rt):
        total = jnp.sum(sq[tab[2 + pair_rows, t]], axis=1, keepdims=True)
        inv[pl.ds(t * tile, tile), :] = jnp.broadcast_to(lax.rsqrt(1.0 + total), (tile, tile))

    for block in blocks_left:
        fetch_block(block)
    gather(fld1, sems1, [functools.partial(mix, c) for c in range(rt)], True, True, 0)
    for c in order:
        rows = pl.ds(c * tile, tile)
        at(fld2, me, c)[...] = (fw1[rows, :] + 2.0 * (acc[rows, :] * inv[rows, :])).astype(BF16)
        emit_own(fld2, sems2, c)
    gather(fld2, sems2, [], True, False, 0)
    out_ref[...] = (base[...] + acc[...] * inv[...]).astype(BF16)
    for kind in range(3):
        remote(f_ref, f_ref, xs.at[kind], xr.at[kind, 0], partner).wait_send()
    drain(fld1, sems1, True, 0)
    drain(fld2, sems2, False, 0)


def fast(features, tile_values, tile_source, tile_target, tile_count, weights, bias_vector):
    slots, tile, _ = tile_values.shape
    rows, cols = features.shape
    rt = rows // tile
    blocks = lax.axis_size("blk")
    levels = blocks // 2
    vmem = pl.BlockSpec(memory_space=pltpu.VMEM)
    hbm = pl.BlockSpec(memory_space=pltpu.HBM)
    dma = pltpu.SemaphoreType.DMA
    gather_sems = [
        dma((levels + 1,)), dma((levels, rt)), dma, dma((levels + 1,)),
    ]
    return pl.pallas_call(
        functools.partial(fast_kernel, levels),
        out_shape=jax.ShapeDtypeStruct((rows, cols), BF16),
        in_specs=[hbm] * 6,
        out_specs=vmem,
        scratch_shapes=[
            pltpu.VMEM((rt, tile, tile), BF16),
            pltpu.VMEM((3, rt, tile, tile), BF16),
            pltpu.VMEM((blocks * (rt - 1), tile, tile), BF16),
            pltpu.VMEM((blocks, tile, tile), BF16),
            pltpu.VMEM((blocks * (rt - 1), tile, tile), BF16),
            pltpu.VMEM((blocks, tile, tile), BF16),
            pltpu.VMEM((slots + 1, tile, tile), BF16),
            pltpu.VMEM((slots + 1, tile, tile), F32),
            pltpu.VMEM((blocks, rows, rows), BF16),
            pltpu.VMEM((3, 4, tile, tile), BF16),
            pltpu.VMEM((rows, tile), F32),
            pltpu.VMEM((rows, tile), F32),
            pltpu.VMEM((rows, tile), F32),
            pltpu.VMEM((rows, tile), F32),
            pltpu.VMEM((8, tile), jnp.int32),
            pltpu.VMEM((8, slots), jnp.int32),
            pltpu.SMEM((8, slots), jnp.int32),
            pltpu.VMEM((1, 4 * cols), F32),
            dma, dma, dma((3,)), dma, dma((4,)), dma((3,)), dma((3, rt)),
        ] + gather_sems + gather_sems,
        compiler_params=pltpu.CompilerParams(collective_id=0, has_side_effects=True, vmem_limit_bytes=58 << 20),
        name="propagate",
    )(
        features.reshape(rt, tile, cols), tile_values, tile_source.reshape(1, -1), tile_target.reshape(1, -1),
        weights, bias_vector.reshape(1, -1),
    )


def per_device(features, tile_values, tile_source, tile_target, tile_count, weights, bias_vector):
    tile_size = tile_values.shape[1]
    slot_total = tile_values.shape[0]
    channels = features.shape[1]
    row_tiles = features.shape[0] // tile_size
    block_rows = row_tiles * tile_size
    block_count = lax.axis_size("blk")
    slot_cap = max(2, (2 * slot_total + block_count - 1) // block_count)
    usable = jnp.arange(slot_total, dtype=jnp.int32) < tile_count[0]
    squares = jnp.einsum(
        "tij,tij->ti", tile_values, tile_values, preferred_element_type=jnp.float32
    )
    squares = jnp.where(usable[:, None], squares, 0.0)
    onehot = (
        (tile_target[:, None] == jnp.arange(row_tiles, dtype=jnp.int32)[None, :]) & usable[:, None]
    ).astype(jnp.float32)
    row_norm = jnp.dot(onehot.T, squares, precision=lax.Precision.HIGHEST)
    inverse = lax.rsqrt(1.0 + row_norm).reshape(-1)
    zero_sum = jnp.zeros((row_tiles, tile_size, channels), jnp.float32)

    def cycle_prop(signal):
        segment = lax.all_gather(signal, "blk", axis=0, tiled=True)
        offset = jnp.int32(0)
        count_rows = segment.shape[0]
        window = min(slot_total, slot_cap * (count_rows // block_rows + 2))
        low_row = tile_source * tile_size
        first_slot = jnp.sum(usable & (low_row + tile_size <= offset))
        end_slot = jnp.sum(usable & (low_row < offset + count_rows))
        start_slot = jnp.minimum(first_slot, slot_total - window)
        slot_ids = start_slot + jnp.arange(window, dtype=jnp.int32)
        in_range = (slot_ids >= first_slot) & (slot_ids < end_slot)
        row_ids = tile_source[:, None] * tile_size + jnp.arange(tile_size, dtype=jnp.int32)[None, :]
        inside = (row_ids >= 0) & (row_ids < count_rows) & in_range[:, None]
        picked = jnp.take(segment, jnp.clip(row_ids, 0, count_rows - 1).reshape(-1), axis=0)
        picked = picked.reshape(window, tile_size, channels)
        picked = jnp.where(inside[:, :, None], picked, jnp.zeros((), segment.dtype))
        product = jnp.einsum(
            "gij,gjc->gic", tile_values, picked, preferred_element_type=jnp.float32
        )
        product = jnp.where(in_range[:, None, None], product, 0.0)
        summed = zero_sum.at[tile_target].add(product)
        return summed.reshape(-1, channels) * inverse[:, None]

    col_start = lax.axis_index("ch") * channels
    bias_part = lax.dynamic_slice_in_dim(bias_vector, col_start, channels, 0)
    w_cols = lax.dynamic_slice_in_dim(weights, col_start, channels, 2)

    def mix_term(order_term, order_index, running):
        w_slice = w_cols[order_index]
        return running + jnp.dot(
            lax.all_gather(order_term, "ch", axis=1, tiled=True),
            w_slice,
            preferred_element_type=jnp.float32,
        )

    result = mix_term(features, 0, jnp.zeros((features.shape[0], channels), jnp.float32))
    first_order = cycle_prop(features).astype(jnp.bfloat16)
    result = mix_term(first_order, 1, result)
    second_order = (2.0 * cycle_prop(first_order) - features.astype(jnp.float32)).astype(
        jnp.bfloat16
    )
    result = mix_term(second_order, 2, result)
    return (result + bias_part[None, :]).astype(jnp.bfloat16)


def solution(mesh):
    dense = mesh.shape["blk"] == 8 and mesh.shape["ch"] == 4
    return jax.shard_map(
        fast if dense else per_device,
        mesh=mesh,
        in_specs=(P("blk", "ch"), P("blk", None, None), P("blk"), P("blk"), P("blk"), P(), P()),
        out_specs=P("blk", "ch"),
        check_vma=False,
    )
```
